32 devices in a mesh: row: 4 (over z), col: 8 (over y, x, core).
Axes of the slice: x: 2, y: 2, z: 4, core: 2. Of those that a mesh axis runs over, the one named last changes fastest.
Arguments:
- grad_first: float32 [4096, 20480], P('row', 'col'), may hold values from -1000 to 1000
- grad_second: float32 [4096, 20480], P('row', 'col'), may hold values from -1000 to 1000
Outputs:
- update: float32 [4096, 20480], P('row', 'col')
The draws below stay inside these ranges and needn't reach their ends.
All inputs are finite; a program needn't handle non-finite values.
Results may differ from the reference program's by a relative error of at most 0.00014.
Values sent between devices are 32-bit elements; how exact they have to be, the bound alone decides.
A program may use at most 128 MiB of HBM per device.

```python
import math
import jax
import jax.numpy as jnp
from jax import lax

D = 4096
FF = 20480
BLOCK = 256
ITERS = 6


def gradient_draw(key, step_number):
    own_key = jax.random.fold_in(key, 101 + step_number)
    row_key = jax.random.fold_in(key, 211)
    col_key = jax.random.fold_in(key, 223)
    upper_scale = 3.0
    entries = jax.random.normal(own_key, (D, FF), jnp.float32)
    row_scale = jnp.exp(jax.random.uniform(row_key, (D,), jnp.float32, 0.0, math.log(upper_scale)))
    col_scale = jnp.exp(jax.random.uniform(col_key, (FF,), jnp.float32, 0.0, math.log(upper_scale)))
    return entries * row_scale[:, None] * col_scale[None, :]


def draw_grad_first(key, part):
    return gradient_draw(key, 0)


def draw_grad_second(key, part):
    return gradient_draw(key, 1)


def setup_inputs(seed: int = 0) -> dict:
    streams_of = jax.random.split(jax.random.key(seed), 3)
    grad_first = draw_grad_first(jax.random.fold_in(streams_of[2], 71), 0)
    grad_second = draw_grad_second(jax.random.fold_in(streams_of[2], 71), 0)
    return dict(grad_first=grad_first, grad_second=grad_second)


damping = 0.001

def batched(left_mat, right_mat):
    return jnp.einsum('kij,kjl->kil', left_mat, right_mat, precision=lax.Precision.HIGHEST)

def newton_roots(statistic):
    width = statistic.shape[-1]
    identity = jnp.eye(width, dtype=jnp.float32)
    damped = statistic + damping * identity
    frob_norm = jnp.sqrt(lax.optimization_barrier(jnp.sum(damped * damped, axis=(1, 2))))
    scaled = damped / frob_norm[:, None, None]
    current = identity[None] * lax.rsqrt(jnp.sqrt(frob_norm))[:, None, None]
    for iteration in range(ITERS):
        factor = (5.0 * identity - scaled) / 4.0
        current = batched(current, factor)
        square = batched(factor, factor)
        scaled = batched(batched(square, square), scaled)
    return current

def reference(grad_first, grad_second):
    left_count = D // BLOCK
    right_count = FF // BLOCK
    left_state = jnp.zeros((left_count, BLOCK, BLOCK), jnp.float32)
    right_state = jnp.zeros((right_count, BLOCK, BLOCK), jnp.float32)
    update = jnp.zeros((D, FF), jnp.float32)
    for gradient in (grad_first, grad_second):
        row_blocks = gradient.reshape(left_count, BLOCK, FF)
        col_blocks = gradient.reshape(D, right_count, BLOCK)
        left_state = left_state + jnp.einsum('bik,bjk->bij', row_blocks, row_blocks, precision=lax.Precision.HIGHEST) / FF
        right_state = right_state + jnp.einsum('kbi,kbj->bij', col_blocks, col_blocks, precision=lax.Precision.HIGHEST) / D
        left_factor = newton_roots(left_state)
        right_factor = newton_roots(right_state)
        halfway = jnp.einsum('bij,bjk->bik', left_factor, row_blocks, precision=lax.Precision.HIGHEST).reshape(D, right_count, BLOCK)
        update = update + jnp.einsum('kbi,bij->kbj', halfway, right_factor, precision=lax.Precision.HIGHEST).reshape(D, FF)
    return update
```

```python
import functools

import jax
import jax.numpy as jnp
from jax import lax
from jax.experimental import pallas as pl
from jax.experimental.pallas import tpu as pltpu
from jax.sharding import PartitionSpec as P

BLOCK = 256
HALF = 128
PACKED = BLOCK + 8
ITERS = 6
damping = 0.001
VMEM_LIMIT = 63 * 1024 * 1024
SLOTS = 3
MESH = pl.DeviceIdType.MESH
NN = (((1,), (0,)), ((), ()))
NT = (((1,), (1,)), ((), ()))


def split(value):
    high = value.astype(jnp.bfloat16)
    low = (value - high.astype(jnp.float32)).astype(jnp.bfloat16)
    return high, low


def dot(left, right, dims=NN):
    return lax.dot_general(left, right, dims, preferred_element_type=jnp.float32)


def product(left, right):
    return dot(
        jnp.concatenate([left[0], left[0], left[1]], axis=1),
        jnp.concatenate([right[0], right[1], right[0]], axis=0),
    )


def indices():
    rows = lax.broadcasted_iota(jnp.int32, (HALF, HALF), 0)
    cols = lax.broadcasted_iota(jnp.int32, (HALF, HALF), 1)
    return rows, cols


def pack(ref, index, block):
    rows, cols = indices()
    first, last = block[:HALF, :HALF], block[HALF:, HALF:]
    ref[index, pl.ds(0, HALF), :] = block[:HALF, HALF:]
    ref[index, pl.ds(HALF, HALF), :] = jnp.where(rows <= cols, first, last)
    diagonal = jnp.sum(jnp.where(rows == cols, last, 0.0), axis=0, keepdims=True)
    ref[index, pl.ds(BLOCK, 8), :] = jnp.broadcast_to(diagonal, (8, HALF))


def unpack(packed):
    rows, cols = indices()
    off = packed[:HALF]
    tile = packed[HALF:BLOCK]
    turned = tile.T
    first = jnp.where(rows <= cols, tile, turned)
    last = jnp.where(rows > cols, tile, jnp.where(rows < cols, turned, packed[BLOCK : BLOCK + 1]))
    return jnp.concatenate(
        [jnp.concatenate([first, off], axis=1), jnp.concatenate([off.T, last], axis=1)], axis=0
    )


def root_of(statistic, scale, x_ref, m_ref):
    rows = lax.broadcasted_iota(jnp.int32, (BLOCK, BLOCK), 0)
    cols = lax.broadcasted_iota(jnp.int32, (BLOCK, BLOCK), 1)
    identity = jnp.where(rows == cols, 1.0, 0.0)

    def factor_of(scaled):
        return (5.0 * identity - scaled) / 4.0

    def advance(factor_parts, scaled):
        square = product(factor_parts, factor_parts)
        square_parts = split(square)
        fourth = product(square_parts, square_parts)
        return product(split(fourth), split(scaled))

    damped = statistic * scale + damping * identity
    total = jnp.sum(jnp.sum(damped * damped, axis=0, keepdims=True), axis=1, keepdims=True)
    norm = jnp.sqrt(total)
    scaled = damped / norm
    factor = factor_of(scaled)
    x_ref[...] = factor * lax.rsqrt(jnp.sqrt(norm))
    m_ref[...] = advance(split(factor), scaled)

    def step(iteration, carry):
        current = m_ref[...]
        parts = split(factor_of(current))
        x_ref[...] = product(split(x_ref[...]), parts)
        m_ref[...] = advance(parts, current)
        return carry

    lax.fori_loop(0, ITERS - 2, step, 0)
    return product(split(x_ref[...]), split(factor_of(m_ref[...])))


def kernel(
    sizes, g1_ref, g2_ref, out_ref, gh, gl, stage, rp, up, dn, rr, lp, lrecv, lr, own, tiles, x_ref, m_ref,
    load_sem, out_sem, up_send, up_recv, dn_send, dn_recv, agu_send, agd_send, ag_recv,
    l_send, l_recv, lag_send, lag_recv,
):
    n, nl, rows, cols = sizes
    lcount, rcount = rows // BLOCK, cols // BLOCK
    M, ML = 2 * rcount, 2 * lcount
    K, KL = pl.cdiv(M, n), pl.cdiv(ML, nl)
    left_scale, right_scale = 1.0 / (cols * nl), 1.0 / (rows * n)
    z, c = lax.axis_index("row"), lax.axis_index("col")
    refs = (g1_ref, g2_ref)

    def load(step, block):
        slot = lax.rem(block, SLOTS)
        columns = pl.ds(pl.multiple_of(block * BLOCK, BLOCK), BLOCK)
        return pltpu.make_async_copy(
            refs[step].at[:, columns], stage.at[step, slot], load_sem.at[step, slot]
        )

    for block in range(min(SLOTS, rcount)):
        for step in range(2):
            load(step, block).start()

    def to_row(source, target, send, recv, row):
        return pltpu.make_async_remote_copy(
            source, target, send, recv, device_id=(row, c), device_id_type=MESH
        )

    def send_up(v, ref):
        return to_row(ref.at[v], up.at[v], up_send.at[v], up_recv.at[v], z + 1)

    def send_down(v, ref):
        return to_row(ref.at[v], dn.at[v], dn_send.at[v], dn_recv.at[v], z - 1)

    def root_up(v):
        return to_row(rr.at[v], rr.at[v], agu_send.at[v], ag_recv.at[v], z + 1)

    def root_down(v):
        return to_row(rr.at[v], rr.at[v], agd_send.at[v], ag_recv.at[v], z - 1)

    def left_out(w):
        return pltpu.make_async_remote_copy(
            lp.at[w], lrecv.at[w // nl, c], l_send.at[w], l_recv.at[w // nl, c],
            device_id=(z, lax.rem(w, nl)), device_id_type=MESH,
        )

    def left_in(kl, source):
        return pltpu.make_async_remote_copy(
            lp.at[0], lrecv.at[kl, source], l_send.at[0], l_recv.at[kl, source],
            device_id=(z, source), device_id_type=MESH,
        )

    def left_root(w, kl, other):
        return pltpu.make_async_remote_copy(
            lr.at[w], lr.at[w], lag_send.at[kl, other], lag_recv.at[w],
            device_id=(z, other), device_id_type=MESH,
        )

    barrier = pltpu.get_barrier_semaphore()

    @pl.when(z > 0)
    def _():
        pl.semaphore_signal(barrier, inc=1, device_id=(z - 1, c), device_id_type=MESH)

    @pl.when(z < n - 1)
    def _():
        pl.semaphore_signal(barrier, inc=1, device_id=(z + 1, c), device_id_type=MESH)

    for d in range(1, nl):
        pl.semaphore_signal(
            barrier, inc=1, device_id=(z, lax.rem(c + d, nl)), device_id_type=MESH
        )
    pl.semaphore_wait(barrier, nl - 1 + jnp.where(z > 0, 1, 0) + jnp.where(z < n - 1, 1, 0))

    def right_stat(block, carry):
        slot = lax.rem(block, SLOTS)
        columns = pl.ds(pl.multiple_of(block * BLOCK, BLOCK), BLOCK)
        total = None
        for step in range(2):
            load(step, block).wait()
            high, low = split(stage[step, slot])
            gh[step, :, columns] = high
            gl[step, :, columns] = low
            turned = high.T
            cross = dot(turned, low)
            part = dot(turned, high) + (cross + cross.T)
            total = part if total is None else total + part
            v = 2 * block + step
            pack(rp, v, total)

        @pl.when(block + SLOTS < rcount)
        def _():
            for step in range(2):
                load(step, block + SLOTS).start()

        for step in range(2):
            v = 2 * block + step
            owner = lax.rem(v, n)

            @pl.when((z == 0) & (owner > 0))
            def _():
                send_up(v, rp).start()

            @pl.when((z == n - 1) & (owner < n - 1))
            def _():
                send_down(v, rp).start()

        return carry

    lax.fori_loop(0, rcount, right_stat, 0)

    def left_stat(block, carry):
        lines = pl.ds(pl.multiple_of(block * BLOCK, BLOCK), BLOCK)
        total = None
        for step in range(2):
            high, low = gh[step, lines, :], gl[step, lines, :]
            cross = dot(high, low, NT)
            part = dot(high, high, NT) + (cross + cross.T)
            total = part if total is None else total + part
            w = 2 * block + step
            pack(lp, w, total)

        for step in range(2):
            w = 2 * block + step

            @pl.when(lax.rem(w, nl) != c)
            def _():
                left_out(w).start()

        return carry

    lax.fori_loop(0, lcount, left_stat, 0)

    def gather(k, d):
        below, above = z - d, z + d

        @pl.when((below >= 0) & (k * n + below < M))
        def _():
            v = k * n + below
            root_up(v).wait_recv()

            @pl.when(z < n - 1)
            def _():
                root_up(v).start()

        @pl.when((above < n) & (k * n + above < M))
        def _():
            v = k * n + above
            root_down(v).wait_recv()

            @pl.when(z > 0)
            def _():
                root_down(v).start()

    def reduce_round(k, slot):
        for d in range(n - 1, 0, -1):
            below, above = z - d, z + d

            @pl.when((above < n) & (z > 0) & (k * n + above < M))
            def _():
                v = k * n + above
                send_up(v, up).wait_recv()
                up[v] = up[v] + rp[v]
                send_up(v, up).start()

            @pl.when((below >= 0) & (z < n - 1) & (k * n + below < M))
            def _():
                v = k * n + below
                send_down(v, dn).wait_recv()
                dn[v] = dn[v] + rp[v]
                send_down(v, dn).start()

        @pl.when(k * n + z < M)
        def _():
            v = k * n + z
            own[slot] = rp[v]

            @pl.when(z > 0)
            def _():
                send_up(v, up).wait_recv()
                own[slot] = own[slot] + up[v]

            @pl.when(z < n - 1)
            def _():
                send_down(v, dn).wait_recv()
                own[slot] = own[slot] + dn[v]

    def left_sum(kl, slot):
        w = kl * nl + c

        @pl.when(w < ML)
        def _():
            own[slot] = lp[w]
            for d in range(1, nl):
                source = lax.rem(c + d, nl)
                left_in(kl, source).wait_recv()
                own[slot] = own[slot] + lrecv[kl, source]

    first_left = max(K - 2, 0)

    def turn(it, carry):
        left = (it >= first_left) & (it < first_left + KL)
        k = jnp.where(it < first_left, it, it - KL)
        kl = it - first_left

        @pl.when(jnp.logical_not(left))
        def _():
            reduce_round(k, it)
            for d in range(1, n):
                @pl.when(k - d >= 0)
                def _():
                    gather(k - d, d)

        @pl.when(left)
        def _():
            left_sum(kl, it)

        exists = jnp.where(left, kl * nl + c < ML, k * n + z < M)

        @pl.when(exists)
        def _():
            scale = jnp.where(left, left_scale, right_scale)
            result = root_of(unpack(own[it]), scale, x_ref, m_ref)
            pack(own, it, result)

            @pl.when(left)
            def _():
                w = kl * nl + c
                lr[w] = own[it]
                for d in range(1, nl):
                    left_root(w, kl, lax.rem(c + d, nl)).start()

            @pl.when(jnp.logical_not(left))
            def _():
                v = k * n + z
                rr[v] = own[it]

                @pl.when(z < n - 1)
                def _():
                    root_up(v).start()

                @pl.when(z > 0)
                def _():
                    root_down(v).start()

        return carry

    lax.fori_loop(0, K + KL, turn, 0)

    def left_arrive(w, carry):
        @pl.when(lax.rem(w, nl) != c)
        def _():
            left_root(w, 0, lax.rem(w, nl)).wait_recv()

        return carry

    lax.fori_loop(0, ML, left_arrive, 0)

    width = cols
    for parts in (2, 3, 5):
        if rcount % parts == 0 and rcount > parts:
            width = cols // parts
            break
    pieces = cols // width

    def left_apply(block, carry):
        lines = pl.ds(pl.multiple_of(block * BLOCK, BLOCK), BLOCK)
        for step in range(2):
            root = split(unpack(lr[2 * block + step]))

            def piece(t, inner):
                columns = pl.ds(pl.multiple_of(t * width, HALF), width)
                high, low = gh[step, lines, columns], gl[step, lines, columns]
                high, low = split(product(root, (high, low)))
                gh[step, lines, columns] = high
                gl[step, lines, columns] = low
                return inner

            lax.fori_loop(0, pieces, piece, 0)

        stage_index = K + block
        for d in range(1, n):
            k = stage_index - d

            @pl.when((k >= 0) & (k < K))
            def _():
                gather(k, d)

        return carry

    lax.fori_loop(0, lcount, left_apply, 0)

    for stage_index in range(K + lcount, K + n - 1):
        for d in range(1, n):
            if 0 <= stage_index - d < K:
                gather(stage_index - d, d)

    def out_copy(block):
        slot = lax.rem(block, 2)
        columns = pl.ds(pl.multiple_of(block * BLOCK, BLOCK), BLOCK)
        return pltpu.make_async_copy(tiles.at[slot], out_ref.at[:, columns], out_sem.at[slot])

    def right_apply(block, carry):
        columns = pl.ds(pl.multiple_of(block * BLOCK, BLOCK), BLOCK)
        slot = lax.rem(block, 2)

        @pl.when(block >= 2)
        def _():
            out_copy(block - 2).wait()

        lefts, rights = [], []
        for step in range(2):
            high, low = split(unpack(rr[2 * block + step]))
            grad_high, grad_low = gh[step, :, columns], gl[step, :, columns]
            lefts += [grad_high, grad_high, grad_low]
            rights += [high, low, high]
        tiles[slot] = dot(jnp.concatenate(lefts, axis=1), jnp.concatenate(rights, axis=0))
        out_copy(block).start()
        return carry

    lax.fori_loop(0, rcount, right_apply, 0)
    for block in range(max(rcount - 2, 0), rcount):
        out_copy(block).wait()

    def drain(v, carry):
        owner = lax.rem(v, n)

        @pl.when((z < n - 1) & (owner > z))
        def _():
            send_up(v, up).wait_send()

        @pl.when((z > 0) & (owner < z))
        def _():
            send_down(v, dn).wait_send()

        @pl.when((z < n - 1) & (owner <= z))
        def _():
            root_up(v).wait_send()

        @pl.when((z > 0) & (owner >= z))
        def _():
            root_down(v).wait_send()

        return carry

    lax.fori_loop(0, M, drain, 0)

    def left_drain(w, carry):
        @pl.when(lax.rem(w, nl) != c)
        def _():
            left_out(w).wait_send()

        @pl.when(lax.rem(w, nl) == c)
        def _():
            for d in range(1, nl):
                left_root(w, w // nl, lax.rem(c + d, nl)).wait_send()

        return carry

    lax.fori_loop(0, ML, left_drain, 0)


def body(n, nl, grad_first, grad_second):
    rows, cols = grad_first.shape
    lcount, rcount = rows // BLOCK, cols // BLOCK
    M, ML = 2 * rcount, 2 * lcount
    K, KL = pl.cdiv(M, n), pl.cdiv(ML, nl)
    f32, bf16 = jnp.float32, jnp.bfloat16
    unit = (PACKED, HALF)
    dma = pltpu.SemaphoreType.DMA
    return pl.pallas_call(
        functools.partial(kernel, (n, nl, rows, cols)),
        in_specs=[pl.BlockSpec(memory_space=pl.ANY)] * 2,
        out_specs=pl.BlockSpec(memory_space=pl.ANY),
        out_shape=jax.ShapeDtypeStruct((rows, cols), f32),
        scratch_shapes=[
            pltpu.VMEM((2, rows, cols), bf16),
            pltpu.VMEM((2, rows, cols), bf16),
            pltpu.VMEM((2, SLOTS, rows, BLOCK), f32),
            pltpu.VMEM((M, *unit), f32),
            pltpu.VMEM((M, *unit), f32),
            pltpu.VMEM((M, *unit), f32),
            pltpu.VMEM((M, *unit), f32),
            pltpu.VMEM((ML, *unit), f32),
            pltpu.VMEM((KL, nl, *unit), f32),
            pltpu.VMEM((ML, *unit), f32),
            pltpu.VMEM((K + KL, *unit), f32),
            pltpu.VMEM((2, rows, BLOCK), f32),
            pltpu.VMEM((BLOCK, BLOCK), f32),
            pltpu.VMEM((BLOCK, BLOCK), f32),
            dma((2, SLOTS)),
            dma((2,)),
            dma((M,)),
            dma((M,)),
            dma((M,)),
            dma((M,)),
            dma((M,)),
            dma((M,)),
            dma((M,)),
            dma((ML,)),
            dma((KL, nl)),
            dma((KL, nl)),
            dma((ML,)),
        ],
        compiler_params=pltpu.CompilerParams(
            collective_id=0, has_side_effects=True, vmem_limit_bytes=VMEM_LIMIT
        ),
    )(grad_first, grad_second)


def solution(mesh):
    spec = P("row", "col")
    return jax.shard_map(
        functools.partial(body, mesh.shape["row"], mesh.shape["col"]),
        mesh=mesh,
        in_specs=(spec, spec),
        out_specs=spec,
        check_vma=False,
    )
```

```python
import functools

import jax
import jax.numpy as jnp
from jax import lax
from jax.experimental import pallas as pl
from jax.experimental.pallas import tpu as pltpu
from jax.sharding import PartitionSpec as P

BLOCK = 256
HALF = 128
PACKED = BLOCK + 8
ITERS = 6
damping = 0.001
VMEM_LIMIT = 63 * 1024 * 1024
SLOTS = 3
MESH = pl.DeviceIdType.MESH
NN = (((1,), (0,)), ((), ()))
NT = (((1,), (1,)), ((), ()))


NOP, STAT, SEND, LEFT, UP, DOWN, GATHER, ROOT, LAPPLY, RAPPLY = range(10)
COST = {STAT: 1.15, LEFT: 1.7, ROOT: 5.4, LAPPLY: 1.55, RAPPLY: 1.12}
START, OVERHEAD, HOP, LINK, SPREAD = 4.0, 0.08, 0.95, 2.785, 11.0


def plan(n, rounds, total, left_units, right_blocks, left_blocks):
    clock = [START] * n
    line, arrival = {}, {}
    programs = [[] for _ in range(n)]
    done = [set() for _ in range(n)]
    spread = [[None, None] for _ in range(n)]

    def post(source, target, key):
        end = max(line.get((source, target), 0.0), clock[source]) + LINK
        line[source, target] = end
        arrival[key] = end + HOP

    def latest(times):
        return None if None in times else max(times, default=0.0)

    def choices(z):
        made = done[z]

        def ready(rank, kind, item, *needs):
            when = latest(needs)
            if when is not None and (kind, item) not in made:
                found.append((when, rank, kind, item))

        def after(kind, item):
            return 0.0 if (kind, item) in made else None

        found = []
        for v in range(total):
            owner = v % n
            if owner > z > 0:
                ready(0, UP, v, after(STAT, v // 2), arrival.get((UP, z, v)))
            if owner < z < n - 1:
                ready(0, DOWN, v, after(STAT, v // 2), arrival.get((DOWN, z, v)))
            if owner != z:
                passed = 0 < z < n - 1
                ready(1 if passed else 8, GATHER, v, arrival.get((GATHER, z, v)))
        stats = [j for j in range(right_blocks) if (STAT, j) not in made]
        for j in stats[:1]:
            ready(2, STAT, j)
        if z in (0, n - 1):
            for k in range(rounds):
                last = min(k * n + n, total) - 1
                ready(0, SEND, k, after(STAT, last // 2))
        if not stats:
            for b in [b for b in range(left_blocks) if (LEFT, b) not in made][:1]:
                ready(3, LEFT, b)
        for k in range(rounds):
            v = k * n + z
            if v < total:
                needs = [after(STAT, v // 2)]
                needs += [arrival.get((UP, z, v))] if z > 0 else []
                needs += [arrival.get((DOWN, z, v))] if z < n - 1 else []
                ready(4, ROOT, k, *needs)
        ready(4, ROOT, rounds, spread[z][0])
        for w in [w for w in range(left_units) if (LAPPLY, w) not in made][:1]:
            ready(5, LAPPLY, w, spread[z][1])
        if (LAPPLY, left_units - 1) in made:
            for j in [j for j in range(right_blocks) if (RAPPLY, j) not in made][:1]:
                needs = [after(ROOT, v // n) if v % n == z else after(GATHER, v) for v in (2 * j, 2 * j + 1)]
                ready(6, RAPPLY, j, *needs)
        return found

    while True:
        options = []
        for z in range(n):
            found = choices(z)
            if found:
                now = [f for f in found if f[0] <= clock[z] + 0.05]
                pick = min(now, key=lambda f: (f[1], f[0])) if now else min(found)
                options.append((max(clock[z], pick[0]), z, pick))
        if not options:
            return programs
        when, z, (_, _, kind, item) = min(options)
        clock[z] = when + OVERHEAD + COST.get(kind, 0.0)
        programs[z].append((kind, item))
        done[z].add((kind, item))
        if kind == SEND:
            units = range(item * n, min(item * n + n, total))
            for v in reversed(units):
                if z == 0 and v % n > 0:
                    post(0, 1, (UP, 1, v))
            for v in units:
                if z == n - 1 and v % n < n - 1:
                    post(z, z - 1, (DOWN, z - 1, v))
        elif kind == LEFT and item == left_blocks - 1:
            spread[z][0] = clock[z] + SPREAD
        elif kind == UP:
            post(z, z + 1, (UP, z + 1, item))
        elif kind == DOWN:
            post(z, z - 1, (DOWN, z - 1, item))
        elif kind == ROOT and item == rounds:
            spread[z][1] = clock[z] + SPREAD
        elif kind in (ROOT, GATHER):
            v = item * n + z if kind == ROOT else item
            if v % n <= z < n - 1:
                post(z, z + 1, (GATHER, z + 1, v))
            if v % n >= z > 0:
                post(z, z - 1, (GATHER, z - 1, v))


def split(value):
    high = value.astype(jnp.bfloat16)
    low = (value - high.astype(jnp.float32)).astype(jnp.bfloat16)
    return high, low


def dot(left, right, dims=NN):
    return lax.dot_general(left, right, dims, preferred_element_type=jnp.float32)


def product(left, right):
    return dot(
        jnp.concatenate([left[0], left[0], left[1]], axis=1),
        jnp.concatenate([right[0], right[1], right[0]], axis=0),
    )


def indices():
    rows = lax.broadcasted_iota(jnp.int32, (HALF, HALF), 0)
    cols = lax.broadcasted_iota(jnp.int32, (HALF, HALF), 1)
    return rows, cols


def pack(ref, index, block):
    rows, cols = indices()
    first, last = block[:HALF, :HALF], block[HALF:, HALF:]
    ref[index, pl.ds(0, HALF), :] = block[:HALF, HALF:]
    ref[index, pl.ds(HALF, HALF), :] = jnp.where(rows <= cols, first, last)
    diagonal = jnp.sum(jnp.where(rows == cols, last, 0.0), axis=0, keepdims=True)
    ref[index, pl.ds(BLOCK, 8), :] = jnp.broadcast_to(diagonal, (8, HALF))


def unpack(packed):
    rows, cols = indices()
    off = packed[:HALF]
    tile = packed[HALF:BLOCK]
    turned = tile.T
    first = jnp.where(rows <= cols, tile, turned)
    last = jnp.where(rows > cols, tile, jnp.where(rows < cols, turned, packed[BLOCK : BLOCK + 1]))
    return jnp.concatenate(
        [jnp.concatenate([first, off], axis=1), jnp.concatenate([off.T, last], axis=1)], axis=0
    )


def root_of(statistic, scale, x_ref, m_ref):
    rows = lax.broadcasted_iota(jnp.int32, (BLOCK, BLOCK), 0)
    cols = lax.broadcasted_iota(jnp.int32, (BLOCK, BLOCK), 1)
    identity = jnp.where(rows == cols, 1.0, 0.0)

    def factor_of(scaled):
        return (5.0 * identity - scaled) / 4.0

    def advance(factor_parts, scaled):
        square = product(factor_parts, factor_parts)
        square_parts = split(square)
        fourth = product(square_parts, square_parts)
        return product(split(fourth), split(scaled))

    damped = statistic * scale + damping * identity
    total = jnp.sum(jnp.sum(damped * damped, axis=0, keepdims=True), axis=1, keepdims=True)
    norm = jnp.sqrt(total)
    scaled = damped / norm
    factor = factor_of(scaled)
    x_ref[...] = factor * lax.rsqrt(jnp.sqrt(norm))
    m_ref[...] = advance(split(factor), scaled)

    def step(iteration, carry):
        current = m_ref[...]
        parts = split(factor_of(current))
        x_ref[...] = product(split(x_ref[...]), parts)
        m_ref[...] = advance(parts, current)
        return carry

    lax.fori_loop(0, ITERS - 2, step, 0)
    return product(split(x_ref[...]), split(factor_of(m_ref[...])))


def kernel(
    sizes, g1_ref, g2_ref, out_ref, gh, gl, stage, rp, up, dn, rr, lp, lrecv, lr, own, tiles, x_ref, m_ref,
    load_sem, out_sem, up_send, up_recv, dn_send, dn_recv, agu_send, agd_send, ag_recv,
    l_send, l_recv, lag_send, lag_recv,
):
    n, nl, rows, cols = sizes
    lcount, rcount = rows // BLOCK, cols // BLOCK
    M, ML = 2 * rcount, 2 * lcount
    K, KL = pl.cdiv(M, n), pl.cdiv(ML, nl)
    left_scale, right_scale = 1.0 / (cols * nl), 1.0 / (rows * n)
    z, c = lax.axis_index("row"), lax.axis_index("col")
    refs = (g1_ref, g2_ref)

    def load(step, block):
        slot = lax.rem(block, SLOTS)
        columns = pl.ds(pl.multiple_of(block * BLOCK, BLOCK), BLOCK)
        return pltpu.make_async_copy(
            refs[step].at[:, columns], stage.at[step, slot], load_sem.at[step, slot]
        )

    for block in range(min(SLOTS, rcount)):
        for step in range(2):
            load(step, block).start()

    def to_row(source, target, send, recv, row):
        return pltpu.make_async_remote_copy(
            source, target, send, recv, device_id=(row, c), device_id_type=MESH
        )

    def send_up(v, ref):
        return to_row(ref.at[v], up.at[v], up_send.at[v], up_recv.at[v], z + 1)

    def send_down(v, ref):
        return to_row(ref.at[v], dn.at[v], dn_send.at[v], dn_recv.at[v], z - 1)

    def root_up(v):
        return to_row(rr.at[v], rr.at[v], agu_send.at[v], ag_recv.at[v], z + 1)

    def root_down(v):
        return to_row(rr.at[v], rr.at[v], agd_send.at[v], ag_recv.at[v], z - 1)

    def left_out(w):
        return pltpu.make_async_remote_copy(
            lp.at[w], lrecv.at[w // nl, c], l_send.at[w], l_recv.at[w // nl, c],
            device_id=(z, lax.rem(w, nl)), device_id_type=MESH,
        )

    def left_in(kl, source):
        return pltpu.make_async_remote_copy(
            lp.at[0], lrecv.at[kl, source], l_send.at[0], l_recv.at[kl, source],
            device_id=(z, source), device_id_type=MESH,
        )

    def left_root(w, kl, other):
        return pltpu.make_async_remote_copy(
            lr.at[w], lr.at[w], lag_send.at[kl, other], lag_recv.at[w],
            device_id=(z, other), device_id_type=MESH,
        )

    barrier = pltpu.get_barrier_semaphore()

    @pl.when(z > 0)
    def _():
        pl.semaphore_signal(barrier, inc=1, device_id=(z - 1, c), device_id_type=MESH)

    @pl.when(z < n - 1)
    def _():
        pl.semaphore_signal(barrier, inc=1, device_id=(z + 1, c), device_id_type=MESH)

    for d in range(1, nl):
        pl.semaphore_signal(
            barrier, inc=1, device_id=(z, lax.rem(c + d, nl)), device_id_type=MESH
        )
    pl.semaphore_wait(barrier, nl - 1 + jnp.where(z > 0, 1, 0) + jnp.where(z < n - 1, 1, 0))

    programs = plan(n, K, M, ML, rcount, lcount)
    length = max(len(program) for program in programs)
    base = 16 * max(M, ML, K + KL, rcount)
    held = max(h for h in (1, 2, 3) if base**h < 2**31)
    words = []
    for start in range(0, length, held):
        values = []
        for program in programs:
            part = (program + [(NOP, 0)] * (length + held))[start : start + held]
            values.append(sum((item * 16 + kind) * base**j for j, (kind, item) in enumerate(part)))
        word = jnp.int32(values[0])
        for row in range(1, n):
            word = jnp.where(z == row, values[row], word)
        words.append(word)

    def code_at(i):
        index, place = i // held, lax.rem(i, held)
        word = words[0]
        for j in range(1, len(words)):
            word = jnp.where(index == j, words[j], word)
        for j in range(1, held):
            word = jnp.where(place >= j, word // base, word)
        return lax.rem(word, base)

    def columns_of(block):
        return pl.ds(pl.multiple_of(block * BLOCK, BLOCK), BLOCK)

    def right_stat(block):
        slot = lax.rem(block, SLOTS)
        columns = columns_of(block)
        total = None
        for step in range(2):
            load(step, block).wait()
            high, low = split(stage[step, slot])
            gh[step, :, columns] = high
            gl[step, :, columns] = low
            turned = high.T
            cross = dot(turned, low)
            part = dot(turned, high) + (cross + cross.T)
            total = part if total is None else total + part
            pack(rp, 2 * block + step, total)

        @pl.when(block + SLOTS < rcount)
        def _():
            for step in range(2):
                load(step, block + SLOTS).start()

    def send_round(k):
        for d in range(1, n):
            up_unit, down_unit = k * n + n - d, k * n + d - 1

            @pl.when((z == 0) & (up_unit < M))
            def _():
                send_up(up_unit, rp).start()

            @pl.when((z == n - 1) & (down_unit < M))
            def _():
                send_down(down_unit, rp).start()

    def left_stat(block):
        lines = columns_of(block)
        total = None
        for step in range(2):
            high, low = gh[step, lines, :], gl[step, lines, :]
            cross = dot(high, low, NT)
            part = dot(high, high, NT) + (cross + cross.T)
            total = part if total is None else total + part
            pack(lp, 2 * block + step, total)

        for step in range(2):
            w = 2 * block + step

            @pl.when(lax.rem(w, nl) != c)
            def _():
                left_out(w).start()

    def relay_up(v):
        send_up(v, up).wait_recv()
        up[v] = up[v] + rp[v]
        send_up(v, up).start()

    def relay_down(v):
        send_down(v, dn).wait_recv()
        dn[v] = dn[v] + rp[v]
        send_down(v, dn).start()

    def gather(v):
        owner = lax.rem(v, n)

        @pl.when(owner < z)
        def _():
            root_up(v).wait_recv()

            @pl.when(z < n - 1)
            def _():
                root_up(v).start()

        @pl.when(owner > z)
        def _():
            root_down(v).wait_recv()

            @pl.when(z > 0)
            def _():
                root_down(v).start()

    def root(k):
        left = k >= K
        kl = k - K
        v, w = k * n + z, kl * nl + c

        @pl.when(jnp.logical_not(left))
        def _():
            own[...] = rp[v]

            @pl.when(z > 0)
            def _():
                send_up(v, up).wait_recv()
                own[...] = own[...] + up[v]

            @pl.when(z < n - 1)
            def _():
                send_down(v, dn).wait_recv()
                own[...] = own[...] + dn[v]

        @pl.when(left & (w < ML))
        def _():
            own[...] = lp[w]
            for d in range(1, nl):
                source = lax.rem(c + d, nl)
                left_in(kl, source).wait_recv()
                own[...] = own[...] + lrecv[kl, source]

        @pl.when(jnp.logical_not(left) | (w < ML))
        def _():
            scale = jnp.where(left, left_scale, right_scale)
            result = root_of(unpack(own[...]), scale, x_ref, m_ref)

            @pl.when(left)
            def _():
                pack(lr, w, result)
                for d in range(1, nl):
                    left_root(w, kl, lax.rem(c + d, nl)).start()

            @pl.when(jnp.logical_not(left))
            def _():
                pack(rr, v, result)

                @pl.when(z < n - 1)
                def _():
                    root_up(v).start()

                @pl.when(z > 0)
                def _():
                    root_down(v).start()

    width = cols
    for parts in (2, 3, 5):
        if rcount % parts == 0 and rcount > parts:
            width = cols // parts
            break
    pieces = cols // width

    def left_apply(w):
        @pl.when(lax.rem(w, nl) != c)
        def _():
            left_root(w, 0, lax.rem(w, nl)).wait_recv()

        step = lax.rem(w, 2)
        lines = columns_of(w // 2)
        factor = split(unpack(lr[w]))

        def piece(t, inner):
            columns = pl.ds(pl.multiple_of(t * width, HALF), width)
            high, low = gh[step, lines, columns], gl[step, lines, columns]
            high, low = split(product(factor, (high, low)))
            gh[step, lines, columns] = high
            gl[step, lines, columns] = low
            return inner

        lax.fori_loop(0, pieces, piece, 0)

    def out_copy(block):
        slot = lax.rem(block, 2)
        return pltpu.make_async_copy(
            tiles.at[slot], out_ref.at[:, columns_of(block)], out_sem.at[slot]
        )

    def right_apply(block):
        columns = columns_of(block)
        slot = lax.rem(block, 2)

        @pl.when(block >= 2)
        def _():
            out_copy(block - 2).wait()

        lefts, rights = [], []
        for step in range(2):
            high, low = split(unpack(rr[2 * block + step]))
            grad_high, grad_low = gh[step, :, columns], gl[step, :, columns]
            lefts += [grad_high, grad_high, grad_low]
            rights += [high, low, high]
        tiles[slot] = dot(jnp.concatenate(lefts, axis=1), jnp.concatenate(rights, axis=0))
        out_copy(block).start()

    work = {
        STAT: right_stat, SEND: send_round, LEFT: left_stat, UP: relay_up, DOWN: relay_down,
        GATHER: gather, ROOT: root, LAPPLY: left_apply, RAPPLY: right_apply,
    }

    def turn(i, carry):
        code = code_at(i)
        kind, item = lax.rem(code, 16), code // 16
        for name, act in work.items():
            @pl.when(kind == name)
            def _():
                act(item)

        return carry

    lax.fori_loop(0, length, turn, 0)
    for block in range(max(rcount - 2, 0), rcount):
        out_copy(block).wait()

    def drain(v, carry):
        owner = lax.rem(v, n)

        @pl.when((z < n - 1) & (owner > z))
        def _():
            send_up(v, up).wait_send()

        @pl.when((z > 0) & (owner < z))
        def _():
            send_down(v, dn).wait_send()

        @pl.when((z < n - 1) & (owner <= z))
        def _():
            root_up(v).wait_send()

        @pl.when((z > 0) & (owner >= z))
        def _():
            root_down(v).wait_send()

        return carry

    lax.fori_loop(0, M, drain, 0)

    def left_drain(w, carry):
        @pl.when(lax.rem(w, nl) != c)
        def _():
            left_out(w).wait_send()

        @pl.when(lax.rem(w, nl) == c)
        def _():
            for d in range(1, nl):
                left_root(w, w // nl, lax.rem(c + d, nl)).wait_send()

        return carry

    lax.fori_loop(0, ML, left_drain, 0)


def body(n, nl, grad_first, grad_second):
    rows, cols = grad_first.shape
    lcount, rcount = rows // BLOCK, cols // BLOCK
    M, ML = 2 * rcount, 2 * lcount
    K, KL = pl.cdiv(M, n), pl.cdiv(ML, nl)
    f32, bf16 = jnp.float32, jnp.bfloat16
    unit = (PACKED, HALF)
    dma = pltpu.SemaphoreType.DMA
    return pl.pallas_call(
        functools.partial(kernel, (n, nl, rows, cols)),
        in_specs=[pl.BlockSpec(memory_space=pl.ANY)] * 2,
        out_specs=pl.BlockSpec(memory_space=pl.ANY),
        out_shape=jax.ShapeDtypeStruct((rows, cols), f32),
        scratch_shapes=[
            pltpu.VMEM((2, rows, cols), bf16),
            pltpu.VMEM((2, rows, cols), bf16),
            pltpu.VMEM((2, SLOTS, rows, BLOCK), f32),
            pltpu.VMEM((M, *unit), f32),
            pltpu.VMEM((M, *unit), f32),
            pltpu.VMEM((M, *unit), f32),
            pltpu.VMEM((M, *unit), f32),
            pltpu.VMEM((ML, *unit), f32),
            pltpu.VMEM((KL, nl, *unit), f32),
            pltpu.VMEM((ML, *unit), f32),
            pltpu.VMEM(unit, f32),
            pltpu.VMEM((2, rows, BLOCK), f32),
            pltpu.VMEM((BLOCK, BLOCK), f32),
            pltpu.VMEM((BLOCK, BLOCK), f32),
            dma((2, SLOTS)),
            dma((2,)),
            dma((M,)),
            dma((M,)),
            dma((M,)),
            dma((M,)),
            dma((M,)),
            dma((M,)),
            dma((M,)),
            dma((ML,)),
            dma((KL, nl)),
            dma((KL, nl)),
            dma((ML,)),
        ],
        compiler_params=pltpu.CompilerParams(
            collective_id=0, has_side_effects=True, vmem_limit_bytes=VMEM_LIMIT
        ),
    )(grad_first, grad_second)


def solution(mesh):
    spec = P("row", "col")
    return jax.shard_map(
        functools.partial(body, mesh.shape["row"], mesh.shape["col"]),
        mesh=mesh,
        in_specs=(spec, spec),
        out_specs=spec,
        check_vma=False,
    )
```

```python
import functools

import jax
import jax.numpy as jnp
from jax import lax
from jax.experimental import pallas as pl
from jax.experimental.pallas import tpu as pltpu
from jax.sharding import PartitionSpec as P

BLOCK = 256
HALF = 128
PACKED = BLOCK + 8
ITERS = 6
damping = 0.001
VMEM_LIMIT = 50 * 1024 * 1024
SLOTS = 3
MESH = pl.DeviceIdType.MESH
NN = (((1,), (0,)), ((), ()))
NT = (((1,), (1,)), ((), ()))


NOP, STAT, SEND, LEFT, UP, DOWN, GATHER, ROOT, LAPPLY, RAPPLY = range(10)
COST = {STAT: 1.15, LEFT: 1.7, ROOT: 5.4, LAPPLY: 1.55, RAPPLY: 1.12}
START, OVERHEAD, HOP, LINK, SPREAD = 2.0, 0.07, 0.95, 2.785, 11.0
FIRST = 2


def plan(n, rounds, total, left_units, right_blocks, left_blocks):
    clock = [START + FIRST * COST[STAT]] * n
    line, arrival = {}, {}
    programs = [[] for _ in range(n)]
    done = [{(STAT, j) for j in range(FIRST)} for _ in range(n)]
    spread = [[None, None] for _ in range(n)]

    def post(source, target, key):
        end = max(line.get((source, target), 0.0), clock[source]) + LINK
        line[source, target] = end
        arrival[key] = end + HOP

    def latest(times):
        return None if None in times else max(times, default=0.0)

    def choices(z):
        made = done[z]

        def ready(rank, kind, item, *needs):
            when = latest(needs)
            if when is not None and (kind, item) not in made:
                found.append((when, rank, kind, item))

        def after(kind, item):
            return 0.0 if (kind, item) in made else None

        found = []
        for v in range(total):
            owner = v % n
            if owner > z > 0:
                ready(0, UP, v, after(STAT, v // 2), arrival.get((UP, z, v)))
            if owner < z < n - 1:
                ready(0, DOWN, v, after(STAT, v // 2), arrival.get((DOWN, z, v)))
            if owner != z and 0 < z < n - 1:
                ready(1, GATHER, v, arrival.get((GATHER, z, v)))
        stats = [j for j in range(right_blocks) if (STAT, j) not in made]
        for j in stats[:1]:
            ready(2, STAT, j)
        if z in (0, n - 1):
            for k in range(rounds):
                last = min(k * n + n, total) - 1
                ready(0, SEND, k, after(STAT, last // 2))
        if not stats:
            for b in [b for b in range(left_blocks) if (LEFT, b) not in made][:1]:
                ready(3, LEFT, b)
        for k in range(rounds):
            v = k * n + z
            if v < total:
                needs = [after(STAT, v // 2)]
                needs += [arrival.get((UP, z, v))] if z > 0 else []
                needs += [arrival.get((DOWN, z, v))] if z < n - 1 else []
                ready(4, ROOT, k, *needs)
        ready(4, ROOT, rounds, spread[z][0])
        for w in [w for w in range(left_units) if (LAPPLY, w) not in made][:1]:
            ready(5, LAPPLY, w, spread[z][1])
        if (LAPPLY, left_units - 1) in made:
            for j in [j for j in range(right_blocks) if (RAPPLY, j) not in made][:1]:
                needs = []
                for v in (2 * j, 2 * j + 1):
                    if v % n == z:
                        needs.append(after(ROOT, v // n))
                    elif 0 < z < n - 1:
                        needs.append(after(GATHER, v))
                    else:
                        needs.append(arrival.get((GATHER, z, v)))
                ready(6, RAPPLY, j, *needs)
        return found

    while True:
        options = []
        for z in range(n):
            found = choices(z)
            if found:
                now = [f for f in found if f[0] <= clock[z] + 0.05]
                pick = min(now, key=lambda f: (f[1], f[0])) if now else min(found)
                options.append((max(clock[z], pick[0]), z, pick))
        if not options:
            return programs
        when, z, (_, _, kind, item) = min(options)
        clock[z] = when + OVERHEAD + COST.get(kind, 0.0)
        programs[z].append((kind, item))
        done[z].add((kind, item))
        if kind == SEND:
            units = range(item * n, min(item * n + n, total))
            for v in reversed(units):
                if z == 0 and v % n > 0:
                    post(0, 1, (UP, 1, v))
            for v in units:
                if z == n - 1 and v % n < n - 1:
                    post(z, z - 1, (DOWN, z - 1, v))
        elif kind == LEFT and item == left_blocks - 1:
            spread[z][0] = clock[z] + SPREAD
        elif kind == UP:
            post(z, z + 1, (UP, z + 1, item))
        elif kind == DOWN:
            post(z, z - 1, (DOWN, z - 1, item))
        elif kind == ROOT and item == rounds:
            spread[z][1] = clock[z] + SPREAD
        elif kind in (ROOT, GATHER):
            v = item * n + z if kind == ROOT else item
            if v % n <= z < n - 1:
                post(z, z + 1, (GATHER, z + 1, v))
            if v % n >= z > 0:
                post(z, z - 1, (GATHER, z - 1, v))


def split(value):
    high = value.astype(jnp.bfloat16)
    low = (value - high.astype(jnp.float32)).astype(jnp.bfloat16)
    return high, low


def dot(left, right, dims=NN):
    return lax.dot_general(left, right, dims, preferred_element_type=jnp.float32)


def product(left, right):
    return dot(
        jnp.concatenate([left[0], left[0], left[1]], axis=1),
        jnp.concatenate([right[0], right[1], right[0]], axis=0),
    )


def indices():
    rows = lax.broadcasted_iota(jnp.int32, (HALF, HALF), 0)
    cols = lax.broadcasted_iota(jnp.int32, (HALF, HALF), 1)
    return rows, cols


def pack(ref, index, block):
    rows, cols = indices()
    first, last = block[:HALF, :HALF], block[HALF:, HALF:]
    ref[index, pl.ds(0, HALF), :] = block[:HALF, HALF:]
    ref[index, pl.ds(HALF, HALF), :] = jnp.where(rows <= cols, first, last)
    diagonal = jnp.sum(jnp.where(rows == cols, last, 0.0), axis=0, keepdims=True)
    ref[index, pl.ds(BLOCK, 8), :] = jnp.broadcast_to(diagonal, (8, HALF))


def unpack(packed):
    rows, cols = indices()
    off = packed[:HALF]
    tile = packed[HALF:BLOCK]
    turned = tile.T
    first = jnp.where(rows <= cols, tile, turned)
    last = jnp.where(rows > cols, tile, jnp.where(rows < cols, turned, packed[BLOCK : BLOCK + 1]))
    return jnp.concatenate(
        [jnp.concatenate([first, off], axis=1), jnp.concatenate([off.T, last], axis=1)], axis=0
    )


def root_of(statistic, scale, x_ref, m_ref):
    rows = lax.broadcasted_iota(jnp.int32, (BLOCK, BLOCK), 0)
    cols = lax.broadcasted_iota(jnp.int32, (BLOCK, BLOCK), 1)
    identity = jnp.where(rows == cols, 1.0, 0.0)

    def factor_of(scaled):
        return (5.0 * identity - scaled) / 4.0

    def advance(factor_parts, scaled):
        square = product(factor_parts, factor_parts)
        square_parts = split(square)
        fourth = product(square_parts, square_parts)
        return product(split(fourth), split(scaled))

    damped = statistic * scale + damping * identity
    total = jnp.sum(jnp.sum(damped * damped, axis=0, keepdims=True), axis=1, keepdims=True)
    norm = jnp.sqrt(total)
    scaled = damped / norm
    factor = factor_of(scaled)
    x_ref[...] = factor * lax.rsqrt(jnp.sqrt(norm))
    m_ref[...] = advance(split(factor), scaled)

    def step(iteration, carry):
        current = m_ref[...]
        parts = split(factor_of(current))
        x_ref[...] = product(split(x_ref[...]), parts)
        m_ref[...] = advance(parts, current)
        return carry

    lax.fori_loop(0, ITERS - 2, step, 0)
    return product(split(x_ref[...]), split(factor_of(m_ref[...])))


def kernel(
    sizes, g1_ref, g2_ref, out_ref, gh, gl, stage, rp, up, dn, rr, lp, lrecv, lr, own, x_ref, m_ref,
    load_sem, up_send, up_recv, dn_send, dn_recv, agu_send, agd_send, ag_recv,
    l_send, l_recv, lag_send, lag_recv,
):
    n, nl, rows, cols = sizes
    lcount, rcount = rows // BLOCK, cols // BLOCK
    M, ML = 2 * rcount, 2 * lcount
    K, KL = pl.cdiv(M, n), pl.cdiv(ML, nl)
    left_scale, right_scale = 1.0 / (cols * nl), 1.0 / (rows * n)
    z, c = lax.axis_index("row"), lax.axis_index("col")
    refs = (g1_ref, g2_ref)

    def load(step, block):
        slot = lax.rem(block, SLOTS)
        columns = pl.ds(pl.multiple_of(block * BLOCK, BLOCK), BLOCK)
        return pltpu.make_async_copy(
            refs[step].at[:, columns], stage.at[step, slot], load_sem.at[step, slot]
        )

    for block in range(min(SLOTS, rcount)):
        for step in range(2):
            load(step, block).start()

    def to_row(source, target, send, recv, row):
        return pltpu.make_async_remote_copy(
            source, target, send, recv, device_id=(row, c), device_id_type=MESH
        )

    def send_up(v, ref):
        return to_row(ref.at[v], up.at[v], up_send, up_recv.at[v], z + 1)

    def send_down(v, ref):
        return to_row(ref.at[v], dn.at[v], dn_send, dn_recv.at[v], z - 1)

    def root_up(v):
        return to_row(rr.at[v], rr.at[v], agu_send, ag_recv.at[v], z + 1)

    def root_down(v):
        return to_row(rr.at[v], rr.at[v], agd_send, ag_recv.at[v], z - 1)

    def left_out(w):
        return pltpu.make_async_remote_copy(
            lp.at[w], lrecv.at[w // nl, c], l_send, l_recv.at[w // nl, c],
            device_id=(z, lax.rem(w, nl)), device_id_type=MESH,
        )

    def left_in(kl, source):
        return pltpu.make_async_remote_copy(
            lp.at[0], lrecv.at[kl, source], l_send, l_recv.at[kl, source],
            device_id=(z, source), device_id_type=MESH,
        )

    def left_root(w, kl, other):
        return pltpu.make_async_remote_copy(
            lr.at[w], lr.at[w], lag_send, lag_recv.at[w],
            device_id=(z, other), device_id_type=MESH,
        )

    barrier = pltpu.get_barrier_semaphore()

    @pl.when(z > 0)
    def _():
        pl.semaphore_signal(barrier, inc=1, device_id=(z - 1, c), device_id_type=MESH)

    @pl.when(z < n - 1)
    def _():
        pl.semaphore_signal(barrier, inc=1, device_id=(z + 1, c), device_id_type=MESH)

    for d in range(1, nl):
        pl.semaphore_signal(
            barrier, inc=1, device_id=(z, lax.rem(c + d, nl)), device_id_type=MESH
        )
    def columns_of(block):
        return pl.ds(pl.multiple_of(block * BLOCK, BLOCK), BLOCK)

    def right_stat(block):
        slot = lax.rem(block, SLOTS)
        columns = columns_of(block)
        total = None
        for step in range(2):
            load(step, block).wait()
            high, low = split(stage[step, slot])
            gh[step, :, columns] = high
            gl[step, :, columns] = low
            turned = high.T
            cross = dot(turned, low)
            part = dot(turned, high) + (cross + cross.T)
            total = part if total is None else total + part
            pack(rp, 2 * block + step, total)

        @pl.when(block + SLOTS < rcount)
        def _():
            for step in range(2):
                load(step, block + SLOTS).start()

    def first_stat(block, carry):
        right_stat(block)
        return carry

    lax.fori_loop(0, FIRST, first_stat, 0)
    pl.semaphore_wait(barrier, nl - 1 + jnp.where(z > 0, 1, 0) + jnp.where(z < n - 1, 1, 0))

    def send_round(k):
        for d in range(1, n):
            up_unit, down_unit = k * n + n - d, k * n + d - 1

            @pl.when((z == 0) & (up_unit < M))
            def _():
                send_up(up_unit, rp).start()

            @pl.when((z == n - 1) & (down_unit < M))
            def _():
                send_down(down_unit, rp).start()

    def left_stat(block):
        lines = columns_of(block)
        total = None
        for step in range(2):
            high, low = gh[step, lines, :], gl[step, lines, :]
            cross = dot(high, low, NT)
            part = dot(high, high, NT) + (cross + cross.T)
            total = part if total is None else total + part
            pack(lp, 2 * block + step, total)

        for step in range(2):
            w = 2 * block + step

            @pl.when(lax.rem(w, nl) != c)
            def _():
                left_out(w).start()

    def relay_up(v):
        send_up(v, up).wait_recv()
        up[v] = up[v] + rp[v]
        send_up(v, up).start()

    def relay_down(v):
        send_down(v, dn).wait_recv()
        dn[v] = dn[v] + rp[v]
        send_down(v, dn).start()

    def gather(v):
        owner = lax.rem(v, n)

        @pl.when(owner < z)
        def _():
            root_up(v).wait_recv()

            @pl.when(z < n - 1)
            def _():
                root_up(v).start()

        @pl.when(owner > z)
        def _():
            root_down(v).wait_recv()

            @pl.when(z > 0)
            def _():
                root_down(v).start()

    def arrive(v):
        @pl.when(((z == 0) | (z == n - 1)) & (lax.rem(v, n) != z))
        def _():
            gather(v)

    def root(k):
        left = k >= K
        kl = k - K
        v, w = k * n + z, kl * nl + c

        @pl.when(jnp.logical_not(left))
        def _():
            own[...] = rp[v]

            @pl.when(z > 0)
            def _():
                send_up(v, up).wait_recv()
                own[...] = own[...] + up[v]

            @pl.when(z < n - 1)
            def _():
                send_down(v, dn).wait_recv()
                own[...] = own[...] + dn[v]

        @pl.when(left & (w < ML))
        def _():
            own[...] = lp[w]
            for d in range(1, nl):
                source = lax.rem(c + d, nl)
                left_in(kl, source).wait_recv()
                own[...] = own[...] + lrecv[kl, source]

        @pl.when(jnp.logical_not(left) | (w < ML))
        def _():
            scale = jnp.where(left, left_scale, right_scale)
            result = root_of(unpack(own[...]), scale, x_ref, m_ref)

            @pl.when(left)
            def _():
                pack(lr, w, result)
                for d in range(1, nl):
                    left_root(w, kl, lax.rem(c + d, nl)).start()

            @pl.when(jnp.logical_not(left))
            def _():
                pack(rr, v, result)

                @pl.when(z < n - 1)
                def _():
                    root_up(v).start()

                @pl.when(z > 0)
                def _():
                    root_down(v).start()

    width = cols
    for parts in (2, 3, 5):
        if rcount % parts == 0 and rcount > parts:
            width = cols // parts
            break
    pieces = cols // width

    def left_apply(w):
        @pl.when(lax.rem(w, nl) != c)
        def _():
            left_root(w, 0, lax.rem(w, nl)).wait_recv()

        step = lax.rem(w, 2)
        lines = columns_of(w // 2)
        factor = split(unpack(lr[w]))

        def piece(t, inner):
            columns = pl.ds(pl.multiple_of(t * width, HALF), width)
            high, low = gh[step, lines, columns], gl[step, lines, columns]
            high, low = split(product(factor, (high, low)))
            gh[step, lines, columns] = high
            gl[step, lines, columns] = low
            return inner

        lax.fori_loop(0, pieces, piece, 0)

    def right_apply(block):
        columns = columns_of(block)
        arrive(2 * block)
        arrive(2 * block + 1)
        lefts, rights = [], []
        for step in range(2):
            high, low = split(unpack(rr[2 * block + step]))
            grad_high, grad_low = gh[step, :, columns], gl[step, :, columns]
            lefts += [grad_high, grad_high, grad_low]
            rights += [high, low, high]
        out_ref[:, columns] = dot(jnp.concatenate(lefts, axis=1), jnp.concatenate(rights, axis=0))

    work = {
        STAT: right_stat, SEND: send_round, LEFT: left_stat, UP: relay_up, DOWN: relay_down,
        GATHER: gather, ROOT: root, LAPPLY: left_apply, RAPPLY: right_apply,
    }
    programs = plan(n, K, M, ML, rcount, lcount)
    digit = 16
    while digit < 16 * max(M, ML, K + KL, rcount):
        digit *= 2
    held = max(h for h in (1, 2, 3) if digit**h < 2**31)
    lists = []
    for program in programs:
        program = program + [(NOP, 0)] * (-len(program) % held)
        codes = [item * 16 + kind for kind, item in program]
        lists.append(
            [sum(code * digit**j for j, code in enumerate(codes[i : i + held])) for i in range(0, len(codes), held)]
        )

    def of_row(values):
        value = jnp.int32(values[0])
        for row in range(1, n):
            value = jnp.where(z == row, values[row], value)
        return value

    longest = max(len(words) for words in lists)
    words = [of_row([w[i] if i < len(w) else 0 for w in lists]) for i in range(longest)]
    last = of_row([len(w) for w in lists])

    def look_up(values, index, width):
        if len(values) == 1:
            return values[0]
        half = width // 2
        low = look_up(values[:half], index, half)
        if len(values) <= half:
            return low
        return jnp.where(lax.rem(index, width) >= half, look_up(values[half:], index, half), low)

    def choose(kind, names):
        if len(names) == 1:
            return work[names[0]]
        middle = (len(names) + 1) // 2
        low, high = choose(kind, names[:middle]), choose(kind, names[middle:])

        def act(item):
            @pl.when(kind < names[middle])
            def _():
                low(item)

            @pl.when(kind >= names[middle])
            def _():
                high(item)

        return act

    def turn(index, carry):
        width = 1
        while width < longest:
            width *= 2

        def task(j, word):
            code = lax.rem(word, digit)
            kind, item = lax.rem(code, 16), lax.div(code, 16)

            @pl.when(kind != NOP)
            def _():
                choose(kind, sorted(work))(item)

            return lax.div(word, digit)

        lax.fori_loop(0, held, task, look_up(words, index, width))
        return carry

    lax.fori_loop(0, last, turn, 0)

    def sent(ref, sem, count):
        if count:
            whole = ref.at[pl.ds(0, count)]
            to_row(whole, whole, sem, ag_recv.at[0], z).wait_send()

    for row in range(n):
        @pl.when(z == row)
        def _():
            owners = [v % n for v in range(M)]
            if row < n - 1:
                sent(up, up_send, sum(owner > row for owner in owners))
                sent(rr, agu_send, sum(owner <= row for owner in owners))
            if row > 0:
                sent(dn, dn_send, sum(owner < row for owner in owners))
                sent(rr, agd_send, sum(owner >= row for owner in owners))

    def left_sent(own_count):
        sent(lp, l_send, ML - own_count)
        sent(lrecv.at[0], lag_send, own_count * (nl - 1))

    if ML % nl:
        @pl.when(c < ML % nl)
        def _():
            left_sent(ML // nl + 1)

        @pl.when(c >= ML % nl)
        def _():
            left_sent(ML // nl)
    else:
        left_sent(ML // nl)


def body(n, nl, grad_first, grad_second):
    rows, cols = grad_first.shape
    lcount, rcount = rows // BLOCK, cols // BLOCK
    M, ML = 2 * rcount, 2 * lcount
    K, KL = pl.cdiv(M, n), pl.cdiv(ML, nl)
    f32, bf16 = jnp.float32, jnp.bfloat16
    unit = (PACKED, HALF)
    dma = pltpu.SemaphoreType.DMA
    return pl.pallas_call(
        functools.partial(kernel, (n, nl, rows, cols)),
        in_specs=[pl.BlockSpec(memory_space=pl.ANY)] * 2,
        out_specs=pl.BlockSpec(memory_space=pltpu.VMEM),
        out_shape=pltpu.VMEM((rows, cols), f32),
        scratch_shapes=[
            pltpu.VMEM((2, rows, cols), bf16),
            pltpu.VMEM((2, rows, cols), bf16),
            pltpu.VMEM((2, SLOTS, rows, BLOCK), f32),
            pltpu.VMEM((M, *unit), f32),
            pltpu.VMEM((M, *unit), f32),
            pltpu.VMEM((M, *unit), f32),
            pltpu.VMEM((M, *unit), f32),
            pltpu.VMEM((ML, *unit), f32),
            pltpu.VMEM((KL, nl, *unit), f32),
            pltpu.VMEM((ML, *unit), f32),
            pltpu.VMEM(unit, f32),
            pltpu.VMEM((BLOCK, BLOCK), f32),
            pltpu.VMEM((BLOCK, BLOCK), f32),
            dma((2, SLOTS)),
            dma,
            dma((M,)),
            dma,
            dma((M,)),
            dma,
            dma,
            dma((M,)),
            dma,
            dma((KL, nl)),
            dma,
            dma((ML,)),
        ],
        compiler_params=pltpu.CompilerParams(
            collective_id=0, has_side_effects=True, vmem_limit_bytes=VMEM_LIMIT
        ),
    )(grad_first, grad_second)


def solution(mesh):
    spec = P("row", "col")
    return jax.shard_map(
        functools.partial(body, mesh.shape["row"], mesh.shape["col"]),
        mesh=mesh,
        in_specs=(spec, spec),
        out_specs=spec,
        check_vma=False,
    )
```

```python
import functools

import jax
import jax.numpy as jnp
from jax import lax
from jax.experimental import pallas as pl
from jax.experimental.pallas import tpu as pltpu
from jax.sharding import PartitionSpec as P

BLOCK = 256
HALF = 128
PACKED = BLOCK + 8
ITERS = 6
damping = 0.001
VMEM_LIMIT = 50 * 1024 * 1024
SLOTS = 3
MESH = pl.DeviceIdType.MESH
NN = (((1,), (0,)), ((), ()))
NT = (((1,), (1,)), ((), ()))


NOP, STAT, SEND, LEFT, UP, DOWN, GATHER, OPEN, STEPS, ROOT, OPEN2, STEPS2, ROOT2, LAPPLY, RAPPLY = range(15)
COST = {
    STAT: 1.12, LEFT: 1.72, OPEN: 1.6, STEPS: 1.6, ROOT: 0.8, OPEN2: 2.1, STEPS2: 2.15, ROOT2: 1.1, LAPPLY: 1.52, RAPPLY: 1.14,
}
START, OVERHEAD, HOP, LINK, SPREAD = 2.3, 0.06, 3.0, 2.785, 9.0
FIRST, SEGMENTS = 2, 2


def plan(n, rounds, total, left_units, right_blocks, left_blocks, groups):
    clock = [START + FIRST * COST[STAT]] * n
    line, arrival = {}, {}
    programs = [[] for _ in range(n)]
    done = [{(STAT, j) for j in range(FIRST)} for _ in range(n)]
    spread = [[None, None] for _ in range(n)]
    opened = [[] for _ in range(n)]

    def post(source, target, key):
        end = max(line.get((source, target), 0.0), clock[source]) + LINK
        line[source, target] = end
        arrival[key] = end + HOP

    def pass_on(z, v):
        if v % n <= z < n - 1:
            post(z, z + 1, (GATHER, z + 1, v))
        if v % n >= z > 0:
            post(z, z - 1, (GATHER, z - 1, v))

    def latest(times):
        return None if None in times else max(times, default=0.0)

    def choices(z):
        made = done[z]

        def ready(rank, kind, item, *needs):
            when = latest(needs)
            if when is not None and (kind, item) not in made:
                found.append((when, rank, kind, item))

        def after(kind, item):
            return 0.0 if (kind, item) in made else None

        found = []
        for v in range(total):
            owner = v % n
            if owner > z > 0:
                ready(0, UP, v, after(STAT, v // 2), arrival.get((UP, z, v)))
            if owner < z < n - 1:
                ready(0, DOWN, v, after(STAT, v // 2), arrival.get((DOWN, z, v)))
            if owner != z and 0 < z < n - 1:
                ready(1, GATHER, v, arrival.get((GATHER, z, v)))
        stats = [j for j in range(right_blocks) if (STAT, j) not in made]
        for j in stats[:1]:
            ready(2, STAT, j)
        if z in (0, n - 1):
            for k in range(rounds):
                last = min(k * n + n, total) - 1
                ready(0, SEND, k, after(STAT, last // 2))
        if not stats:
            for b in [b for b in range(left_blocks) if (LEFT, b) not in made][:1]:
                ready(3, LEFT, b)
        def closed(group):
            return after(ROOT if len(group) == 1 else ROOT2, group) == 0.0

        for group in groups:
            needs = []
            for k in group:
                v = k * n + z
                if k == rounds:
                    needs.append(spread[z][0])
                elif v < total:
                    needs.append(after(STAT, v // 2))
                    needs += [arrival.get((UP, z, v))] if z > 0 else []
                    needs += [arrival.get((DOWN, z, v))] if z < n - 1 else []
            if all(closed(other) for other in opened[z]):
                ready(4, OPEN if len(group) == 1 else OPEN2, group, *needs)
        for group in opened[z]:
            if not closed(group):
                middle, end = (STEPS, ROOT) if len(group) == 1 else (STEPS2, ROOT2)
                steps = [i for i in range(SEGMENTS) if (middle, (i, group)) not in made]
                for i in steps[:1]:
                    ready(3.5, middle, (i, group))
                if not steps:
                    ready(3.5, end, group)

        def rooted(k):
            return 0.0 if any(k in group and closed(group) for group in groups) else None

        for w in [w for w in range(left_units) if (LAPPLY, w) not in made][:1]:
            ready(5, LAPPLY, w, spread[z][1])
        if (LAPPLY, left_units - 1) in made:
            for j in [j for j in range(right_blocks) if (RAPPLY, j) not in made][:1]:
                needs = []
                for v in (2 * j, 2 * j + 1):
                    if v % n == z:
                        needs.append(rooted(v // n))
                    elif 0 < z < n - 1:
                        needs.append(after(GATHER, v))
                    else:
                        needs.append(arrival.get((GATHER, z, v)))
                ready(6, RAPPLY, j, *needs)
        return found

    while True:
        options = []
        for z in range(n):
            found = choices(z)
            if found:
                now = [f for f in found if f[0] <= clock[z] + 0.05]
                pick = min(now, key=lambda f: (f[1], f[0])) if now else min(found)
                options.append((max(clock[z], pick[0]), z, pick))
        if not options:
            return programs
        when, z, (_, _, kind, item) = min(options)
        clock[z] = when + OVERHEAD + COST.get(kind, 0.0)
        done[z].add((kind, item))
        if kind in (OPEN, OPEN2):
            opened[z].append(item)
        pairs = [group for group in groups if len(group) == 2]
        number = item
        if kind in (OPEN, ROOT):
            number = item[0]
        elif kind in (OPEN2, ROOT2):
            number = pairs.index(item)
        elif kind in (STEPS, STEPS2):
            number = 0
        programs[z].append((kind, number))
        if kind == SEND:
            units = range(item * n, min(item * n + n, total))
            for v in reversed(units):
                if z == 0 and v % n > 0:
                    post(0, 1, (UP, 1, v))
            for v in units:
                if z == n - 1 and v % n < n - 1:
                    post(z, z - 1, (DOWN, z - 1, v))
        elif kind == LEFT and item == left_blocks - 1:
            spread[z][0] = clock[z] + SPREAD
        elif kind == UP:
            post(z, z + 1, (UP, z + 1, item))
        elif kind == DOWN:
            post(z, z - 1, (DOWN, z - 1, item))
        elif kind == GATHER:
            pass_on(z, item)
        elif kind in (ROOT, ROOT2):
            for k in item:
                if k == rounds:
                    spread[z][1] = clock[z] + SPREAD
                elif k * n + z < total:
                    pass_on(z, k * n + z)


def split(value):
    high = value.astype(jnp.bfloat16)
    low = (value - high.astype(jnp.float32)).astype(jnp.bfloat16)
    return high, low


def dot(left, right, dims=NN):
    return lax.dot_general(left, right, dims, preferred_element_type=jnp.float32)


def product(left, right):
    return dot(
        jnp.concatenate([left[0], left[0], left[1]], axis=1),
        jnp.concatenate([right[0], right[1], right[0]], axis=0),
    )


def indices():
    rows = lax.broadcasted_iota(jnp.int32, (HALF, HALF), 0)
    cols = lax.broadcasted_iota(jnp.int32, (HALF, HALF), 1)
    return rows, cols


def pack(ref, index, block):
    rows, cols = indices()
    first, last = block[:HALF, :HALF], block[HALF:, HALF:]
    ref[index, pl.ds(0, HALF), :] = block[:HALF, HALF:]
    ref[index, pl.ds(HALF, HALF), :] = jnp.where(rows <= cols, first, last)
    diagonal = jnp.sum(jnp.where(rows == cols, last, 0.0), axis=0, keepdims=True)
    ref[index, pl.ds(BLOCK, 8), :] = jnp.broadcast_to(diagonal, (8, HALF))


def unpack(packed):
    rows, cols = indices()
    off = packed[:HALF]
    tile = packed[HALF:BLOCK]
    turned = tile.T
    first = jnp.where(rows <= cols, tile, turned)
    last = jnp.where(rows > cols, tile, jnp.where(rows < cols, turned, packed[BLOCK : BLOCK + 1]))
    return jnp.concatenate(
        [jnp.concatenate([first, off], axis=1), jnp.concatenate([off.T, last], axis=1)], axis=0
    )


def groups_of(rounds):
    return [(k,) for k in range(rounds - 2)] + [(rounds,), (rounds - 2,), (rounds - 1,)] if rounds > 3 else [(k,) for k in range(rounds + 1)]


def factor_of(scaled):
    rows = lax.broadcasted_iota(jnp.int32, (BLOCK, BLOCK), 0)
    cols = lax.broadcasted_iota(jnp.int32, (BLOCK, BLOCK), 1)
    return jnp.where(rows == cols, 1.25, 0.0) - scaled * 0.25


def advance_all(parts, scaled):
    squares = [split(product(p, p)) for p in parts]
    fourths = [product(p, p) for p in squares]
    return [product(split(f), split(m)) for f, m in zip(fourths, scaled)]


def root_open(statistics, scales, x_ref, m_ref):
    rows = lax.broadcasted_iota(jnp.int32, (BLOCK, BLOCK), 0)
    cols = lax.broadcasted_iota(jnp.int32, (BLOCK, BLOCK), 1)
    scaled, factors = [], []
    for i, (statistic, scale) in enumerate(zip(statistics, scales)):
        damped = statistic * scale + jnp.where(rows == cols, damping, 0.0)
        total = jnp.sum(jnp.sum(damped * damped, axis=0, keepdims=True), axis=1, keepdims=True)
        norm = jnp.sqrt(total)
        scaled.append(damped / norm)
        factors.append(factor_of(scaled[i]))
        x_ref[i] = factors[i] * lax.rsqrt(jnp.sqrt(norm))
    for i, value in enumerate(advance_all([split(f) for f in factors], scaled)):
        m_ref[i] = value


def root_steps(chains, count, x_ref, m_ref):
    def step(iteration, carry):
        scaled = [m_ref[i] for i in range(chains)]
        parts = [split(factor_of(m)) for m in scaled]
        for i in range(chains):
            x_ref[i] = product(split(x_ref[i]), parts[i])
        for i, value in enumerate(advance_all(parts, scaled)):
            m_ref[i] = value
        return carry

    lax.fori_loop(0, count, step, 0)


def root_close(chains, x_ref, m_ref):
    return [product(split(x_ref[i]), split(factor_of(m_ref[i]))) for i in range(chains)]


def kernel(
    sizes, g1_ref, g2_ref, out_ref, gh, gl, stage, rp, up, dn, rr, lp, lrecv, lr, own, x_ref, m_ref,
    load_sem, up_send, up_recv, dn_send, dn_recv, agu_send, agd_send, ag_recv,
    l_send, l_recv, lag_send, lag_recv,
):
    n, nl, rows, cols = sizes
    lcount, rcount = rows // BLOCK, cols // BLOCK
    M, ML = 2 * rcount, 2 * lcount
    K, KL = pl.cdiv(M, n), pl.cdiv(ML, nl)
    left_scale, right_scale = 1.0 / (cols * nl), 1.0 / (rows * n)
    z, c = lax.axis_index("row"), lax.axis_index("col")
    refs = (g1_ref, g2_ref)
    groups = groups_of(K)
    pairs = [group for group in groups if len(group) == 2]

    def load(step, block):
        slot = lax.rem(block, SLOTS)
        columns = pl.ds(pl.multiple_of(block * BLOCK, BLOCK), BLOCK)
        return pltpu.make_async_copy(
            refs[step].at[:, columns], stage.at[step, slot], load_sem.at[step, slot]
        )

    for block in range(min(SLOTS, rcount)):
        for step in range(2):
            load(step, block).start()

    def to_row(source, target, send, recv, row):
        return pltpu.make_async_remote_copy(
            source, target, send, recv, device_id=(row, c), device_id_type=MESH
        )

    def send_up(v, ref):
        return to_row(ref.at[v], up.at[v], up_send, up_recv.at[v], z + 1)

    def send_down(v, ref):
        return to_row(ref.at[v], dn.at[v], dn_send, dn_recv.at[v], z - 1)

    def root_up(v):
        return to_row(rr.at[v], rr.at[v], agu_send, ag_recv.at[v], z + 1)

    def root_down(v):
        return to_row(rr.at[v], rr.at[v], agd_send, ag_recv.at[v], z - 1)

    def left_out(w):
        return pltpu.make_async_remote_copy(
            lp.at[w], lrecv.at[w // nl, c], l_send, l_recv.at[w // nl, c],
            device_id=(z, lax.rem(w, nl)), device_id_type=MESH,
        )

    def left_in(kl, source):
        return pltpu.make_async_remote_copy(
            lp.at[0], lrecv.at[kl, source], l_send, l_recv.at[kl, source],
            device_id=(z, source), device_id_type=MESH,
        )

    def left_root(w, kl, other):
        return pltpu.make_async_remote_copy(
            lr.at[w], lr.at[w], lag_send, lag_recv.at[w],
            device_id=(z, other), device_id_type=MESH,
        )

    barrier = pltpu.get_barrier_semaphore()

    @pl.when(z > 0)
    def _():
        pl.semaphore_signal(barrier, inc=1, device_id=(z - 1, c), device_id_type=MESH)

    @pl.when(z < n - 1)
    def _():
        pl.semaphore_signal(barrier, inc=1, device_id=(z + 1, c), device_id_type=MESH)

    for d in range(1, nl):
        pl.semaphore_signal(
            barrier, inc=1, device_id=(z, lax.rem(c + d, nl)), device_id_type=MESH
        )
    def columns_of(block):
        return pl.ds(pl.multiple_of(block * BLOCK, BLOCK), BLOCK)

    def right_stat(block):
        slot = lax.rem(block, SLOTS)
        columns = columns_of(block)
        total = None
        for step in range(2):
            load(step, block).wait()
            high, low = split(stage[step, slot])
            gh[step, :, columns] = high
            gl[step, :, columns] = low
            turned = high.T
            cross = dot(turned, low)
            part = dot(turned, high) + (cross + cross.T)
            total = part if total is None else total + part
            pack(rp, 2 * block + step, total)

        @pl.when(block + SLOTS < rcount)
        def _():
            for step in range(2):
                load(step, block + SLOTS).start()

    def first_stat(block, carry):
        right_stat(block)
        return carry

    lax.fori_loop(0, FIRST, first_stat, 0)
    pl.semaphore_wait(barrier, nl - 1 + jnp.where(z > 0, 1, 0) + jnp.where(z < n - 1, 1, 0))

    def send_round(k):
        for d in range(1, n):
            up_unit, down_unit = k * n + n - d, k * n + d - 1

            @pl.when((z == 0) & (up_unit < M))
            def _():
                send_up(up_unit, rp).start()

            @pl.when((z == n - 1) & (down_unit < M))
            def _():
                send_down(down_unit, rp).start()

    def left_stat(block):
        lines = columns_of(block)
        total = None
        for step in range(2):
            high, low = gh[step, lines, :], gl[step, lines, :]
            cross = dot(high, low, NT)
            part = dot(high, high, NT) + (cross + cross.T)
            total = part if total is None else total + part
            pack(lp, 2 * block + step, total)

        for step in range(2):
            w = 2 * block + step

            @pl.when(lax.rem(w, nl) != c)
            def _():
                left_out(w).start()

    def relay_up(v):
        send_up(v, up).wait_recv()
        up[v] = up[v] + rp[v]
        send_up(v, up).start()

    def relay_down(v):
        send_down(v, dn).wait_recv()
        dn[v] = dn[v] + rp[v]
        send_down(v, dn).start()

    def gather(v):
        owner = lax.rem(v, n)

        @pl.when(owner < z)
        def _():
            root_up(v).wait_recv()

            @pl.when(z < n - 1)
            def _():
                root_up(v).start()

        @pl.when(owner > z)
        def _():
            root_down(v).wait_recv()

            @pl.when(z > 0)
            def _():
                root_down(v).start()

    def arrive(v):
        @pl.when(((z == 0) | (z == n - 1)) & (lax.rem(v, n) != z))
        def _():
            gather(v)

    def collect(k, slot):
        left = k >= K
        kl = k - K
        v, w = k * n + z, kl * nl + c

        @pl.when(jnp.logical_not(left) & (v < M))
        def _():
            own[slot] = rp[v]

            @pl.when(z > 0)
            def _():
                send_up(v, up).wait_recv()
                own[slot] = own[slot] + up[v]

            @pl.when(z < n - 1)
            def _():
                send_down(v, dn).wait_recv()
                own[slot] = own[slot] + dn[v]

        @pl.when(left & (w < ML))
        def _():
            own[slot] = lp[w]
            for d in range(1, nl):
                source = lax.rem(c + d, nl)
                left_in(kl, source).wait_recv()
                own[slot] = own[slot] + lrecv[kl, source]

    def scale_of(k):
        return jnp.where(k >= K, left_scale, right_scale)

    def deliver(k, result):
        left = k >= K
        kl = k - K
        v, w = k * n + z, kl * nl + c

        @pl.when(left & (w < ML))
        def _():
            pack(lr, w, result)
            for d in range(1, nl):
                left_root(w, kl, lax.rem(c + d, nl)).start()

        @pl.when(jnp.logical_not(left) & (v < M))
        def _():
            pack(rr, v, result)

            @pl.when(z < n - 1)
            def _():
                root_up(v).start()

            @pl.when(z > 0)
            def _():
                root_down(v).start()

    def members(item):
        first, second = jnp.int32(pairs[0][0]), jnp.int32(pairs[0][1])
        for j in range(1, len(pairs)):
            first = jnp.where(item == j, pairs[j][0], first)
            second = jnp.where(item == j, pairs[j][1], second)
        return first, second

    def opening(ks):
        for slot, k in enumerate(ks):
            collect(k, slot)
        root_open([unpack(own[slot]) for slot in range(len(ks))], [scale_of(k) for k in ks], x_ref, m_ref)

    def closing(ks):
        for k, result in zip(ks, root_close(len(ks), x_ref, m_ref)):
            deliver(k, result)

    def open_one(k):
        opening((k,))

    def steps_one(item):
        root_steps(1, (ITERS - 2) // SEGMENTS, x_ref, m_ref)

    def close_one(k):
        closing((k,))

    def open_two(item):
        opening(members(item))

    def steps_two(item):
        root_steps(2, (ITERS - 2) // SEGMENTS, x_ref, m_ref)

    def close_two(item):
        closing(members(item))

    width = cols
    for parts in (2, 3, 5):
        if rcount % parts == 0 and rcount > parts:
            width = cols // parts
            break
    pieces = cols // width

    def left_apply(w):
        @pl.when(lax.rem(w, nl) != c)
        def _():
            left_root(w, 0, lax.rem(w, nl)).wait_recv()

        step = lax.rem(w, 2)
        lines = columns_of(w // 2)
        factor = split(unpack(lr[w]))

        def piece(t, inner):
            columns = pl.ds(pl.multiple_of(t * width, HALF), width)
            high, low = gh[step, lines, columns], gl[step, lines, columns]
            high, low = split(product(factor, (high, low)))
            gh[step, lines, columns] = high
            gl[step, lines, columns] = low
            return inner

        lax.fori_loop(0, pieces, piece, 0)

    def right_apply(block):
        columns = columns_of(block)
        arrive(2 * block)
        arrive(2 * block + 1)
        lefts, rights = [], []
        for step in range(2):
            high, low = split(unpack(rr[2 * block + step]))
            grad_high, grad_low = gh[step, :, columns], gl[step, :, columns]
            lefts += [grad_high, grad_high, grad_low]
            rights += [high, low, high]
        out_ref[:, columns] = dot(jnp.concatenate(lefts, axis=1), jnp.concatenate(rights, axis=0))

    work = {
        STAT: right_stat, SEND: send_round, LEFT: left_stat, UP: relay_up, DOWN: relay_down,
        GATHER: gather, OPEN: open_one, STEPS: steps_one, ROOT: close_one,
        OPEN2: open_two, STEPS2: steps_two, ROOT2: close_two, LAPPLY: left_apply, RAPPLY: right_apply,
    }
    programs = plan(n, K, M, ML, rcount, lcount, groups)
    used = sorted({kind for program in programs for kind, _ in program} & set(work))
    digit = 16
    while digit < 16 * max(M, ML, K + KL, rcount):
        digit *= 2
    held = max(h for h in (1, 2, 3) if digit**h < 2**31)
    lists = []
    for program in programs:
        program = program + [(NOP, 0)] * (-len(program) % held)
        codes = [item * 16 + kind for kind, item in program]
        lists.append(
            [sum(code * digit**j for j, code in enumerate(codes[i : i + held])) for i in range(0, len(codes), held)]
        )

    def of_row(values):
        value = jnp.int32(values[0])
        for row in range(1, n):
            value = jnp.where(z == row, values[row], value)
        return value

    longest = max(len(words) for words in lists)
    words = [of_row([w[i] if i < len(w) else 0 for w in lists]) for i in range(longest)]
    last = of_row([len(w) for w in lists])

    def look_up(values, index, width):
        if len(values) == 1:
            return values[0]
        half = width // 2
        low = look_up(values[:half], index, half)
        if len(values) <= half:
            return low
        return jnp.where(lax.rem(index, width) >= half, look_up(values[half:], index, half), low)

    def choose(kind, names):
        if len(names) == 1:
            return work[names[0]]
        middle = (len(names) + 1) // 2
        low, high = choose(kind, names[:middle]), choose(kind, names[middle:])

        def act(item):
            @pl.when(kind < names[middle])
            def _():
                low(item)

            @pl.when(kind >= names[middle])
            def _():
                high(item)

        return act

    def turn(index, carry):
        width = 1
        while width < longest:
            width *= 2

        def task(j, word):
            code = lax.rem(word, digit)
            kind, item = lax.rem(code, 16), lax.div(code, 16)

            @pl.when(kind != NOP)
            def _():
                choose(kind, used)(item)

            return lax.div(word, digit)

        lax.fori_loop(0, held, task, look_up(words, index, width))
        return carry

    lax.fori_loop(0, last, turn, 0)

    def sent(ref, sem, count):
        if count:
            whole = ref.at[pl.ds(0, count)]
            to_row(whole, whole, sem, ag_recv.at[0], z).wait_send()

    for row in range(n):
        @pl.when(z == row)
        def _():
            owners = [v % n for v in range(M)]
            if row < n - 1:
                sent(up, up_send, sum(owner > row for owner in owners))
                sent(rr, agu_send, sum(owner <= row for owner in owners))
            if row > 0:
                sent(dn, dn_send, sum(owner < row for owner in owners))
                sent(rr, agd_send, sum(owner >= row for owner in owners))

    def left_sent(own_count):
        sent(lp, l_send, ML - own_count)
        sent(lrecv.at[0], lag_send, own_count * (nl - 1))

    if ML % nl:
        @pl.when(c < ML % nl)
        def _():
            left_sent(ML // nl + 1)

        @pl.when(c >= ML % nl)
        def _():
            left_sent(ML // nl)
    else:
        left_sent(ML // nl)


def body(n, nl, grad_first, grad_second):
    rows, cols = grad_first.shape
    lcount, rcount = rows // BLOCK, cols // BLOCK
    M, ML = 2 * rcount, 2 * lcount
    K, KL = pl.cdiv(M, n), pl.cdiv(ML, nl)
    f32, bf16 = jnp.float32, jnp.bfloat16
    unit = (PACKED, HALF)
    dma = pltpu.SemaphoreType.DMA
    return pl.pallas_call(
        functools.partial(kernel, (n, nl, rows, cols)),
        in_specs=[pl.BlockSpec(memory_space=pl.ANY)] * 2,
        out_specs=pl.BlockSpec(memory_space=pltpu.VMEM),
        out_shape=pltpu.VMEM((rows, cols), f32),
        scratch_shapes=[
            pltpu.VMEM((2, rows, cols), bf16),
            pltpu.VMEM((2, rows, cols), bf16),
            pltpu.VMEM((2, SLOTS, rows, BLOCK), f32),
            pltpu.VMEM((M, *unit), f32),
            pltpu.VMEM((M, *unit), f32),
            pltpu.VMEM((M, *unit), f32),
            pltpu.VMEM((M, *unit), f32),
            pltpu.VMEM((ML, *unit), f32),
            pltpu.VMEM((KL, nl, *unit), f32),
            pltpu.VMEM((ML, *unit), f32),
            pltpu.VMEM((2, *unit), f32),
            pltpu.VMEM((2, BLOCK, BLOCK), f32),
            pltpu.VMEM((2, BLOCK, BLOCK), f32),
            dma((2, SLOTS)),
            dma,
            dma((M,)),
            dma,
            dma((M,)),
            dma,
            dma,
            dma((M,)),
            dma,
            dma((KL, nl)),
            dma,
            dma((ML,)),
        ],
        compiler_params=pltpu.CompilerParams(
            collective_id=0, has_side_effects=True, vmem_limit_bytes=VMEM_LIMIT
        ),
    )(grad_first, grad_second)


def solution(mesh):
    spec = P("row", "col")
    return jax.shard_map(
        functools.partial(body, mesh.shape["row"], mesh.shape["col"]),
        mesh=mesh,
        in_specs=(spec, spec),
        out_specs=spec,
        check_vma=False,
    )
```

```python
import functools

import jax
import jax.numpy as jnp
from jax import lax
from jax.experimental import pallas as pl
from jax.experimental.pallas import tpu as pltpu
from jax.sharding import PartitionSpec as P

BLOCK = 256
HALF = 128
PACKED = BLOCK + 8
ITERS = 6
damping = 0.001
VMEM_LIMIT = 50 * 1024 * 1024
SLOTS = 3
MESH = pl.DeviceIdType.MESH
NN = (((1,), (0,)), ((), ()))
NT = (((1,), (1,)), ((), ()))


NOP, STAT, SEND, LEFT, UP, DOWN, GATHER, OPEN, STEPS, ROOT, OPEN2, STEPS2, ROOT2, LAPPLY, RAPPLY = range(15)
COST = {
    STAT: 1.12, LEFT: 1.72, OPEN: 1.6, STEPS: 1.6, ROOT: 0.8, OPEN2: 2.1, STEPS2: 2.15, ROOT2: 1.1, LAPPLY: 1.52, RAPPLY: 1.14,
}
START, OVERHEAD, HOP, LINK, SPREAD = 2.3, 0.06, 3.0, 2.785, 9.0
FIRST, SEGMENTS = 2, 2
MARGIN = 3.0


def plan(n, rounds, total, left_units, right_blocks, left_blocks, groups):
    clock = [START + FIRST * COST[STAT]] * n
    line, arrival = {}, {}
    programs = [[] for _ in range(n)]
    done = [{(STAT, j) for j in range(FIRST)} for _ in range(n)]
    spread = [[None, None] for _ in range(n)]
    opened = [[] for _ in range(n)]

    def post(source, target, key):
        end = max(line.get((source, target), 0.0), clock[source]) + LINK
        line[source, target] = end
        arrival[key] = end + HOP

    def pass_on(z, v):
        if v % n <= z < n - 1:
            post(z, z + 1, (GATHER, z + 1, v))
        if v % n >= z > 0:
            post(z, z - 1, (GATHER, z - 1, v))

    def latest(times):
        return None if None in times else max(times, default=0.0)

    def choices(z):
        made = done[z]

        def ready(rank, kind, item, *needs):
            when = latest(needs)
            if when is not None and (kind, item) not in made:
                found.append((when, rank, kind, item))

        def after(kind, item):
            return 0.0 if (kind, item) in made else None

        found = []
        for v in range(total):
            owner = v % n
            if owner > z > 0:
                ready(0, UP, v, after(STAT, v // 2), arrival.get((UP, z, v)))
            if owner < z < n - 1:
                ready(0, DOWN, v, after(STAT, v // 2), arrival.get((DOWN, z, v)))
            if owner != z and 0 < z < n - 1:
                ready(1, GATHER, v, arrival.get((GATHER, z, v)))
        stats = [j for j in range(right_blocks) if (STAT, j) not in made]
        for j in stats[:1]:
            ready(2, STAT, j)
        if z in (0, n - 1):
            for k in range(rounds):
                last = min(k * n + n, total) - 1
                ready(0, SEND, k, after(STAT, last // 2))
        if not stats:
            for b in [b for b in range(left_blocks) if (LEFT, b) not in made][:1]:
                ready(3, LEFT, b)
        def late(when):
            return when if when is None or 0 < z < n - 1 else when + MARGIN

        def closed(group):
            return after(ROOT if len(group) == 1 else ROOT2, group) == 0.0

        for group in groups:
            needs = []
            for k in group:
                v = k * n + z
                if k == rounds:
                    needs.append(spread[z][0])
                elif v < total:
                    needs.append(after(STAT, v // 2))
                    needs += [late(arrival.get((UP, z, v)))] if z > 0 else []
                    needs += [late(arrival.get((DOWN, z, v)))] if z < n - 1 else []
            if all(closed(other) for other in opened[z]):
                ready(4, OPEN if len(group) == 1 else OPEN2, group, *needs)
        for group in opened[z]:
            if not closed(group):
                middle, end = (STEPS, ROOT) if len(group) == 1 else (STEPS2, ROOT2)
                steps = [i for i in range(SEGMENTS) if (middle, (i, group)) not in made]
                for i in steps[:1]:
                    ready(3.5, middle, (i, group))
                if not steps:
                    ready(3.5, end, group)

        def rooted(k):
            return 0.0 if any(k in group and closed(group) for group in groups) else None

        for w in [w for w in range(left_units) if (LAPPLY, w) not in made][:1]:
            ready(5, LAPPLY, w, spread[z][1])
        if (LAPPLY, left_units - 1) in made:
            for j in [j for j in range(right_blocks) if (RAPPLY, j) not in made][:1]:
                needs = []
                for v in (2 * j, 2 * j + 1):
                    if v % n == z:
                        needs.append(rooted(v // n))
                    elif 0 < z < n - 1:
                        needs.append(after(GATHER, v))
                    else:
                        needs.append(arrival.get((GATHER, z, v)))
                ready(6, RAPPLY, j, *needs)
        return found

    while True:
        options = []
        for z in range(n):
            found = choices(z)
            if found:
                now = [f for f in found if f[0] <= clock[z] + 0.05]
                pick = min(now, key=lambda f: (f[1], f[0])) if now else min(found)
                options.append((max(clock[z], pick[0]), z, pick))
        if not options:
            return programs
        when, z, (_, _, kind, item) = min(options)
        clock[z] = when + OVERHEAD + COST.get(kind, 0.0)
        done[z].add((kind, item))
        if kind in (OPEN, OPEN2):
            opened[z].append(item)
        pairs = [group for group in groups if len(group) == 2]
        number = item
        if kind in (OPEN, ROOT):
            number = item[0]
        elif kind in (OPEN2, ROOT2):
            number = pairs.index(item)
        elif kind in (STEPS, STEPS2):
            number = 0
        programs[z].append((kind, number))
        if kind == SEND:
            units = range(item * n, min(item * n + n, total))
            for v in reversed(units):
                if z == 0 and v % n > 0:
                    post(0, 1, (UP, 1, v))
            for v in units:
                if z == n - 1 and v % n < n - 1:
                    post(z, z - 1, (DOWN, z - 1, v))
        elif kind == LEFT and item == left_blocks - 1:
            spread[z][0] = clock[z] + SPREAD
        elif kind == UP:
            post(z, z + 1, (UP, z + 1, item))
        elif kind == DOWN:
            post(z, z - 1, (DOWN, z - 1, item))
        elif kind == GATHER:
            pass_on(z, item)
        elif kind in (ROOT, ROOT2):
            for k in item:
                if k == rounds:
                    spread[z][1] = clock[z] + SPREAD
                elif k * n + z < total:
                    pass_on(z, k * n + z)


def split(value):
    high = value.astype(jnp.bfloat16)
    low = (value - high.astype(jnp.float32)).astype(jnp.bfloat16)
    return high, low


def dot(left, right, dims=NN):
    return lax.dot_general(left, right, dims, preferred_element_type=jnp.float32)


def product(left, right):
    return dot(
        jnp.concatenate([left[0], left[0], left[1]], axis=1),
        jnp.concatenate([right[0], right[1], right[0]], axis=0),
    )


def indices():
    rows = lax.broadcasted_iota(jnp.int32, (HALF, HALF), 0)
    cols = lax.broadcasted_iota(jnp.int32, (HALF, HALF), 1)
    return rows, cols


def pack(ref, index, block):
    rows, cols = indices()
    first, last = block[:HALF, :HALF], block[HALF:, HALF:]
    ref[index, pl.ds(0, HALF), :] = block[:HALF, HALF:]
    ref[index, pl.ds(HALF, HALF), :] = jnp.where(rows <= cols, first, last)
    diagonal = jnp.sum(jnp.where(rows == cols, last, 0.0), axis=0, keepdims=True)
    ref[index, pl.ds(BLOCK, 8), :] = jnp.broadcast_to(diagonal, (8, HALF))


def unpack(packed):
    rows, cols = indices()
    off = packed[:HALF]
    tile = packed[HALF:BLOCK]
    turned = tile.T
    first = jnp.where(rows <= cols, tile, turned)
    last = jnp.where(rows > cols, tile, jnp.where(rows < cols, turned, packed[BLOCK : BLOCK + 1]))
    return jnp.concatenate(
        [jnp.concatenate([first, off], axis=1), jnp.concatenate([off.T, last], axis=1)], axis=0
    )


def groups_of(rounds):
    return [(k,) for k in range(rounds - 2)] + [(rounds,), (rounds - 2,), (rounds - 1,)] if rounds > 3 else [(k,) for k in range(rounds + 1)]


def factor_of(scaled):
    rows = lax.broadcasted_iota(jnp.int32, (BLOCK, BLOCK), 0)
    cols = lax.broadcasted_iota(jnp.int32, (BLOCK, BLOCK), 1)
    return jnp.where(rows == cols, 1.25, 0.0) - scaled * 0.25


def advance_all(parts, scaled):
    squares = [split(product(p, p)) for p in parts]
    fourths = [product(p, p) for p in squares]
    return [product(split(f), split(m)) for f, m in zip(fourths, scaled)]


def root_open(statistics, scales, x_ref, m_ref):
    rows = lax.broadcasted_iota(jnp.int32, (BLOCK, BLOCK), 0)
    cols = lax.broadcasted_iota(jnp.int32, (BLOCK, BLOCK), 1)
    scaled, factors = [], []
    for i, (statistic, scale) in enumerate(zip(statistics, scales)):
        damped = statistic * scale + jnp.where(rows == cols, damping, 0.0)
        total = jnp.sum(jnp.sum(damped * damped, axis=0, keepdims=True), axis=1, keepdims=True)
        norm = jnp.sqrt(total)
        scaled.append(damped / norm)
        factors.append(factor_of(scaled[i]))
        x_ref[i] = factors[i] * lax.rsqrt(jnp.sqrt(norm))
    for i, value in enumerate(advance_all([split(f) for f in factors], scaled)):
        m_ref[i] = value


def root_steps(chains, count, x_ref, m_ref):
    def step(iteration, carry):
        scaled = [m_ref[i] for i in range(chains)]
        parts = [split(factor_of(m)) for m in scaled]
        for i in range(chains):
            x_ref[i] = product(split(x_ref[i]), parts[i])
        for i, value in enumerate(advance_all(parts, scaled)):
            m_ref[i] = value
        return carry

    for iteration in range(count):
        step(iteration, 0)


def root_close(chains, x_ref, m_ref):
    return [product(split(x_ref[i]), split(factor_of(m_ref[i]))) for i in range(chains)]


def kernel(
    sizes, g1_ref, g2_ref, out_ref, gh, gl, stage, rp, up, dn, rr, lp, lrecv, lr, own, x_ref, m_ref,
    load_sem, up_send, up_recv, dn_send, dn_recv, agu_send, agd_send, ag_recv,
    l_send, l_recv, lag_send, lag_recv,
):
    n, nl, rows, cols = sizes
    lcount, rcount = rows // BLOCK, cols // BLOCK
    M, ML = 2 * rcount, 2 * lcount
    K, KL = pl.cdiv(M, n), pl.cdiv(ML, nl)
    left_scale, right_scale = 1.0 / (cols * nl), 1.0 / (rows * n)
    z, c = lax.axis_index("row"), lax.axis_index("col")
    refs = (g1_ref, g2_ref)
    groups = groups_of(K)
    pairs = [group for group in groups if len(group) == 2]

    def load(step, block):
        slot = lax.rem(block, SLOTS)
        columns = pl.ds(pl.multiple_of(block * BLOCK, BLOCK), BLOCK)
        return pltpu.make_async_copy(
            refs[step].at[:, columns], stage.at[step, slot], load_sem.at[step, slot]
        )

    for block in range(min(SLOTS, rcount)):
        for step in range(2):
            load(step, block).start()

    def to_row(source, target, send, recv, row):
        return pltpu.make_async_remote_copy(
            source, target, send, recv, device_id=(row, c), device_id_type=MESH
        )

    def send_up(v, ref):
        return to_row(ref.at[v], up.at[v], up_send, up_recv.at[v], z + 1)

    def send_down(v, ref):
        return to_row(ref.at[v], dn.at[v], dn_send, dn_recv.at[v], z - 1)

    def root_up(v):
        return to_row(rr.at[v], rr.at[v], agu_send, ag_recv.at[v], z + 1)

    def root_down(v):
        return to_row(rr.at[v], rr.at[v], agd_send, ag_recv.at[v], z - 1)

    def left_out(w):
        return pltpu.make_async_remote_copy(
            lp.at[w], lrecv.at[w // nl, c], l_send, l_recv.at[w // nl, c],
            device_id=(z, lax.rem(w, nl)), device_id_type=MESH,
        )

    def left_in(kl, source):
        return pltpu.make_async_remote_copy(
            lp.at[0], lrecv.at[kl, source], l_send, l_recv.at[kl, source],
            device_id=(z, source), device_id_type=MESH,
        )

    def left_root(w, kl, other):
        return pltpu.make_async_remote_copy(
            lr.at[w], lr.at[w], lag_send, lag_recv.at[w],
            device_id=(z, other), device_id_type=MESH,
        )

    barrier = pltpu.get_barrier_semaphore()

    @pl.when(z > 0)
    def _():
        pl.semaphore_signal(barrier, inc=1, device_id=(z - 1, c), device_id_type=MESH)

    @pl.when(z < n - 1)
    def _():
        pl.semaphore_signal(barrier, inc=1, device_id=(z + 1, c), device_id_type=MESH)

    for d in range(1, nl):
        pl.semaphore_signal(
            barrier, inc=1, device_id=(z, lax.rem(c + d, nl)), device_id_type=MESH
        )
    def columns_of(block):
        return pl.ds(pl.multiple_of(block * BLOCK, BLOCK), BLOCK)

    def right_stat(block):
        slot = lax.rem(block, SLOTS)
        columns = columns_of(block)
        total = None
        for step in range(2):
            load(step, block).wait()
            high, low = split(stage[step, slot])
            gh[step, :, columns] = high
            gl[step, :, columns] = low
            turned = high.T
            cross = dot(turned, low)
            part = dot(turned, high) + (cross + cross.T)
            total = part if total is None else total + part
            pack(rp, 2 * block + step, total)

        @pl.when(block + SLOTS < rcount)
        def _():
            for step in range(2):
                load(step, block + SLOTS).start()

    def first_stat(block, carry):
        right_stat(block)
        return carry

    lax.fori_loop(0, FIRST, first_stat, 0)
    pl.semaphore_wait(barrier, nl - 1 + jnp.where(z > 0, 1, 0) + jnp.where(z < n - 1, 1, 0))

    def send_round(k):
        for d in range(1, n):
            up_unit, down_unit = k * n + n - d, k * n + d - 1

            @pl.when((z == 0) & (up_unit < M))
            def _():
                send_up(up_unit, rp).start()

            @pl.when((z == n - 1) & (down_unit < M))
            def _():
                send_down(down_unit, rp).start()

    def left_stat(block):
        lines = columns_of(block)
        total = None
        for step in range(2):
            high, low = gh[step, lines, :], gl[step, lines, :]
            cross = dot(high, low, NT)
            part = dot(high, high, NT) + (cross + cross.T)
            total = part if total is None else total + part
            pack(lp, 2 * block + step, total)

        for step in range(2):
            w = 2 * block + step

            @pl.when(lax.rem(w, nl) != c)
            def _():
                left_out(w).start()

    def relay_up(v):
        send_up(v, up).wait_recv()
        up[v] = up[v] + rp[v]
        send_up(v, up).start()

    def relay_down(v):
        send_down(v, dn).wait_recv()
        dn[v] = dn[v] + rp[v]
        send_down(v, dn).start()

    def gather(v):
        owner = lax.rem(v, n)

        @pl.when(owner < z)
        def _():
            root_up(v).wait_recv()

            @pl.when(z < n - 1)
            def _():
                root_up(v).start()

        @pl.when(owner > z)
        def _():
            root_down(v).wait_recv()

            @pl.when(z > 0)
            def _():
                root_down(v).start()

    def arrive(v):
        @pl.when(((z == 0) | (z == n - 1)) & (lax.rem(v, n) != z))
        def _():
            gather(v)

    def collect(k, slot):
        left = k >= K
        kl = k - K
        v, w = k * n + z, kl * nl + c

        @pl.when(jnp.logical_not(left) & (v < M))
        def _():
            own[slot] = rp[v]

            @pl.when(z > 0)
            def _():
                send_up(v, up).wait_recv()
                own[slot] = own[slot] + up[v]

            @pl.when(z < n - 1)
            def _():
                send_down(v, dn).wait_recv()
                own[slot] = own[slot] + dn[v]

        @pl.when(left & (w < ML))
        def _():
            own[slot] = lp[w]
            for d in range(1, nl):
                source = lax.rem(c + d, nl)
                left_in(kl, source).wait_recv()
                own[slot] = own[slot] + lrecv[kl, source]

    def scale_of(k):
        return jnp.where(k >= K, left_scale, right_scale)

    def deliver(k, result):
        left = k >= K
        kl = k - K
        v, w = k * n + z, kl * nl + c

        @pl.when(left & (w < ML))
        def _():
            pack(lr, w, result)
            for d in range(1, nl):
                left_root(w, kl, lax.rem(c + d, nl)).start()

        @pl.when(jnp.logical_not(left) & (v < M))
        def _():
            pack(rr, v, result)

            @pl.when(z < n - 1)
            def _():
                root_up(v).start()

            @pl.when(z > 0)
            def _():
                root_down(v).start()

    def members(item):
        first, second = jnp.int32(pairs[0][0]), jnp.int32(pairs[0][1])
        for j in range(1, len(pairs)):
            first = jnp.where(item == j, pairs[j][0], first)
            second = jnp.where(item == j, pairs[j][1], second)
        return first, second

    def opening(ks):
        for slot, k in enumerate(ks):
            collect(k, slot)
        root_open([unpack(own[slot]) for slot in range(len(ks))], [scale_of(k) for k in ks], x_ref, m_ref)

    def closing(ks):
        for k, result in zip(ks, root_close(len(ks), x_ref, m_ref)):
            deliver(k, result)

    def open_one(k):
        opening((k,))

    def steps_one(item):
        root_steps(1, (ITERS - 2) // SEGMENTS, x_ref, m_ref)

    def close_one(k):
        closing((k,))

    def open_two(item):
        opening(members(item))

    def steps_two(item):
        root_steps(2, (ITERS - 2) // SEGMENTS, x_ref, m_ref)

    def close_two(item):
        closing(members(item))

    width, pieces = cols, 1

    def left_apply(w):
        @pl.when(lax.rem(w, nl) != c)
        def _():
            left_root(w, 0, lax.rem(w, nl)).wait_recv()

        step = lax.rem(w, 2)
        lines = columns_of(w // 2)
        factor = split(unpack(lr[w]))

        def piece(t, inner):
            columns = pl.ds(pl.multiple_of(t * width, HALF), width)
            high, low = gh[step, lines, columns], gl[step, lines, columns]
            high, low = split(product(factor, (high, low)))
            gh[step, lines, columns] = high
            gl[step, lines, columns] = low
            return inner

        lax.fori_loop(0, pieces, piece, 0)

    def right_apply(block):
        columns = columns_of(block)
        arrive(2 * block)
        arrive(2 * block + 1)
        lefts, rights = [], []
        for step in range(2):
            high, low = split(unpack(rr[2 * block + step]))
            grad_high, grad_low = gh[step, :, columns], gl[step, :, columns]
            lefts += [grad_high, grad_high, grad_low]
            rights += [high, low, high]
        out_ref[:, columns] = dot(jnp.concatenate(lefts, axis=1), jnp.concatenate(rights, axis=0))

    work = {
        STAT: right_stat, SEND: send_round, LEFT: left_stat, UP: relay_up, DOWN: relay_down,
        GATHER: gather, OPEN: open_one, STEPS: steps_one, ROOT: close_one,
        OPEN2: open_two, STEPS2: steps_two, ROOT2: close_two, LAPPLY: left_apply, RAPPLY: right_apply,
    }
    programs = plan(n, K, M, ML, rcount, lcount, groups)
    used = sorted({kind for program in programs for kind, _ in program} & set(work))
    digit = 16
    while digit < 16 * max(M, ML, K + KL, rcount):
        digit *= 2
    held = max(h for h in (1, 2, 3) if digit**h < 2**31)
    lists = []
    for program in programs:
        program = program + [(NOP, 0)] * (-len(program) % held)
        codes = [item * 16 + kind for kind, item in program]
        lists.append(
            [sum(code * digit**j for j, code in enumerate(codes[i : i + held])) for i in range(0, len(codes), held)]
        )

    def of_row(values):
        value = jnp.int32(values[0])
        for row in range(1, n):
            value = jnp.where(z == row, values[row], value)
        return value

    longest = max(len(words) for words in lists)
    words = [of_row([w[i] if i < len(w) else 0 for w in lists]) for i in range(longest)]
    last = of_row([len(w) for w in lists])

    def look_up(values, index, width):
        if len(values) == 1:
            return values[0]
        half = width // 2
        low = look_up(values[:half], index, half)
        if len(values) <= half:
            return low
        return jnp.where(lax.rem(index, width) >= half, look_up(values[half:], index, half), low)

    def choose(kind, names):
        if len(names) == 1:
            return work[names[0]]
        middle = (len(names) + 1) // 2
        low, high = choose(kind, names[:middle]), choose(kind, names[middle:])

        def act(item):
            @pl.when(kind < names[middle])
            def _():
                low(item)

            @pl.when(kind >= names[middle])
            def _():
                high(item)

        return act

    def turn(index, carry):
        width = 1
        while width < longest:
            width *= 2

        def task(j, word):
            code = lax.rem(word, digit)
            kind, item = lax.rem(code, 16), lax.div(code, 16)

            @pl.when(kind != NOP)
            def _():
                choose(kind, used)(item)

            return lax.div(word, digit)

        lax.fori_loop(0, held, task, look_up(words, index, width))
        return carry

    lax.fori_loop(0, last, turn, 0)

    def sent(ref, sem, count):
        if count:
            whole = ref.at[pl.ds(0, count)]
            to_row(whole, whole, sem, ag_recv.at[0], z).wait_send()

    for row in range(n):
        @pl.when(z == row)
        def _():
            owners = [v % n for v in range(M)]
            if row < n - 1:
                sent(up, up_send, sum(owner > row for owner in owners))
                sent(rr, agu_send, sum(owner <= row for owner in owners))
            if row > 0:
                sent(dn, dn_send, sum(owner < row for owner in owners))
                sent(rr, agd_send, sum(owner >= row for owner in owners))

    def left_sent(own_count):
        sent(lp, l_send, ML - own_count)
        sent(lrecv.at[0], lag_send, own_count * (nl - 1))

    if ML % nl:
        @pl.when(c < ML % nl)
        def _():
            left_sent(ML // nl + 1)

        @pl.when(c >= ML % nl)
        def _():
            left_sent(ML // nl)
    else:
        left_sent(ML // nl)


def body(n, nl, grad_first, grad_second):
    rows, cols = grad_first.shape
    lcount, rcount = rows // BLOCK, cols // BLOCK
    M, ML = 2 * rcount, 2 * lcount
    K, KL = pl.cdiv(M, n), pl.cdiv(ML, nl)
    f32, bf16 = jnp.float32, jnp.bfloat16
    unit = (PACKED, HALF)
    dma = pltpu.SemaphoreType.DMA
    return pl.pallas_call(
        functools.partial(kernel, (n, nl, rows, cols)),
        in_specs=[pl.BlockSpec(memory_space=pl.ANY)] * 2,
        out_specs=pl.BlockSpec(memory_space=pltpu.VMEM),
        out_shape=pltpu.VMEM((rows, cols), f32),
        scratch_shapes=[
            pltpu.VMEM((2, rows, cols), bf16),
            pltpu.VMEM((2, rows, cols), bf16),
            pltpu.VMEM((2, SLOTS, rows, BLOCK), f32),
            pltpu.VMEM((M, *unit), f32),
            pltpu.VMEM((M, *unit), f32),
            pltpu.VMEM((M, *unit), f32),
            pltpu.VMEM((M, *unit), f32),
            pltpu.VMEM((ML, *unit), f32),
            pltpu.VMEM((KL, nl, *unit), f32),
            pltpu.VMEM((ML, *unit), f32),
            pltpu.VMEM((2, *unit), f32),
            pltpu.VMEM((2, BLOCK, BLOCK), f32),
            pltpu.VMEM((2, BLOCK, BLOCK), f32),
            dma((2, SLOTS)),
            dma,
            dma((M,)),
            dma,
            dma((M,)),
            dma,
            dma,
            dma((M,)),
            dma,
            dma((KL, nl)),
            dma,
            dma((ML,)),
        ],
        compiler_params=pltpu.CompilerParams(
            collective_id=0, has_side_effects=True, vmem_limit_bytes=VMEM_LIMIT
        ),
    )(grad_first, grad_second)


def solution(mesh):
    spec = P("row", "col")
    return jax.shard_map(
        functools.partial(body, mesh.shape["row"], mesh.shape["col"]),
        mesh=mesh,
        in_specs=(spec, spec),
        out_specs=spec,
        check_vma=False,
    )
```

```python
import functools

import jax
import jax.numpy as jnp
from jax import lax
from jax.experimental import pallas as pl
from jax.experimental.pallas import tpu as pltpu
from jax.sharding import PartitionSpec as P

BLOCK = 256
HALF = 128
PACKED = BLOCK + 8
ITERS = 6
damping = 0.001
VMEM_LIMIT = 50 * 1024 * 1024
SLOTS = 3
MESH = pl.DeviceIdType.MESH
NN = (((1,), (0,)), ((), ()))
NT = (((1,), (1,)), ((), ()))


NOP, STAT, SEND, LEFT, UP, DOWN, GATHER, OPEN, STEPS, ROOT, OPEN2, STEPS2, ROOT2, LAPPLY, RAPPLY = range(15)
COST = {
    STAT: 1.12, LEFT: 1.72, OPEN: 1.6, STEPS: 1.6, ROOT: 0.8, OPEN2: 2.1, STEPS2: 2.15, ROOT2: 1.1, LAPPLY: 1.52, RAPPLY: 1.14,
}
START, OVERHEAD, HOP, LINK, SPREAD = 2.3, 0.06, 3.0, 2.785, 9.0
FIRST, SEGMENTS = 2, 2
MARGIN = 3.0


def plan(n, rounds, total, left_units, right_blocks, left_blocks, groups):
    clock = [START + FIRST * COST[STAT]] * n
    line, arrival = {}, {}
    programs = [[] for _ in range(n)]
    done = [{(STAT, j) for j in range(FIRST)} for _ in range(n)]
    spread = [[None, None] for _ in range(n)]
    opened = [[] for _ in range(n)]

    def post(source, target, key):
        end = max(line.get((source, target), 0.0), clock[source]) + LINK
        line[source, target] = end
        arrival[key] = end + HOP

    def pass_on(z, v):
        if v % n <= z < n - 1:
            post(z, z + 1, (GATHER, z + 1, v))
        if v % n >= z > 0:
            post(z, z - 1, (GATHER, z - 1, v))

    def latest(times):
        return None if None in times else max(times, default=0.0)

    def choices(z):
        made = done[z]

        def ready(rank, kind, item, *needs):
            when = latest(needs)
            if when is not None and (kind, item) not in made:
                found.append((when, rank, kind, item))

        def after(kind, item):
            return 0.0 if (kind, item) in made else None

        found = []
        for v in range(total):
            owner = v % n
            if owner > z > 0:
                ready(0, UP, v, after(STAT, v // 2), arrival.get((UP, z, v)))
            if owner < z < n - 1:
                ready(0, DOWN, v, after(STAT, v // 2), arrival.get((DOWN, z, v)))
            if owner != z and 0 < z < n - 1:
                ready(1, GATHER, v, arrival.get((GATHER, z, v)))
        stats = [j for j in range(right_blocks) if (STAT, j) not in made]
        for j in stats[:1]:
            ready(2, STAT, j)
        if z in (0, n - 1):
            for k in range(rounds):
                last = min(k * n + n, total) - 1
                ready(0, SEND, k, after(STAT, last // 2))
        if not stats:
            for b in [b for b in range(left_blocks) if (LEFT, b) not in made][:1]:
                ready(3, LEFT, b)
        def late(when):
            return when if when is None or 0 < z < n - 1 else when + MARGIN

        def closed(group):
            return after(ROOT if len(group) == 1 else ROOT2, group) == 0.0

        for group in groups:
            needs = []
            for k in group:
                v = k * n + z
                if k == rounds:
                    needs.append(spread[z][0])
                elif v < total:
                    needs.append(after(STAT, v // 2))
                    needs += [late(arrival.get((UP, z, v)))] if z > 0 else []
                    needs += [late(arrival.get((DOWN, z, v)))] if z < n - 1 else []
            if all(closed(other) for other in opened[z]):
                ready(4, OPEN if len(group) == 1 else OPEN2, group, *needs)
        for group in opened[z]:
            if not closed(group):
                middle, end = (STEPS, ROOT) if len(group) == 1 else (STEPS2, ROOT2)
                steps = [i for i in range(SEGMENTS) if (middle, (i, group)) not in made]
                for i in steps[:1]:
                    ready(3.5, middle, (i, group))
                if not steps:
                    ready(3.5, end, group)

        def rooted(k):
            return 0.0 if any(k in group and closed(group) for group in groups) else None

        for w in [w for w in range(left_units) if (LAPPLY, w) not in made][:1]:
            ready(5, LAPPLY, w, spread[z][1])
        if (LAPPLY, left_units - 1) in made:
            for j in [j for j in range(right_blocks) if (RAPPLY, j) not in made][:1]:
                needs = []
                for v in (2 * j, 2 * j + 1):
                    if v % n == z:
                        needs.append(rooted(v // n))
                    elif 0 < z < n - 1:
                        needs.append(after(GATHER, v))
                    else:
                        needs.append(arrival.get((GATHER, z, v)))
                ready(6, RAPPLY, j, *needs)
        return found

    while True:
        options = []
        for z in range(n):
            found = choices(z)
            if found:
                now = [f for f in found if f[0] <= clock[z] + 0.05]
                pick = min(now, key=lambda f: (f[1], f[0])) if now else min(found)
                options.append((max(clock[z], pick[0]), z, pick))
        if not options:
            return programs
        when, z, (_, _, kind, item) = min(options)
        clock[z] = when + OVERHEAD + COST.get(kind, 0.0)
        done[z].add((kind, item))
        if kind in (OPEN, OPEN2):
            opened[z].append(item)
        pairs = [group for group in groups if len(group) == 2]
        number = item
        if kind in (OPEN, ROOT):
            number = item[0]
        elif kind in (OPEN2, ROOT2):
            number = pairs.index(item)
        elif kind in (STEPS, STEPS2):
            number = 0
        programs[z].append((kind, number))
        if kind == SEND:
            units = range(item * n, min(item * n + n, total))
            for v in reversed(units):
                if z == 0 and v % n > 0:
                    post(0, 1, (UP, 1, v))
            for v in units:
                if z == n - 1 and v % n < n - 1:
                    post(z, z - 1, (DOWN, z - 1, v))
        elif kind == LEFT and item == left_blocks - 1:
            spread[z][0] = clock[z] + SPREAD
        elif kind == UP:
            post(z, z + 1, (UP, z + 1, item))
        elif kind == DOWN:
            post(z, z - 1, (DOWN, z - 1, item))
        elif kind == GATHER:
            pass_on(z, item)
        elif kind in (ROOT, ROOT2):
            for k in item:
                if k == rounds:
                    spread[z][1] = clock[z] + SPREAD
                elif k * n + z < total:
                    pass_on(z, k * n + z)


def split(value):
    high = value.astype(jnp.bfloat16)
    low = (value - high.astype(jnp.float32)).astype(jnp.bfloat16)
    return high, low


def dot(left, right, dims=NN):
    return lax.dot_general(left, right, dims, preferred_element_type=jnp.float32)


def product(left, right):
    return dot(
        jnp.concatenate([left[0], left[0], left[1]], axis=1),
        jnp.concatenate([right[0], right[1], right[0]], axis=0),
    )


def indices():
    rows = lax.broadcasted_iota(jnp.int32, (HALF, HALF), 0)
    cols = lax.broadcasted_iota(jnp.int32, (HALF, HALF), 1)
    return rows, cols


def pack(ref, index, block):
    rows, cols = indices()
    first, last = block[:HALF, :HALF], block[HALF:, HALF:]
    ref[index, pl.ds(0, HALF), :] = block[:HALF, HALF:]
    ref[index, pl.ds(HALF, HALF), :] = jnp.where(rows <= cols, first, last)
    diagonal = jnp.sum(jnp.where(rows == cols, last, 0.0), axis=0, keepdims=True)
    ref[index, pl.ds(BLOCK, 8), :] = jnp.broadcast_to(diagonal, (8, HALF))


def unpack(packed):
    rows, cols = indices()
    off = packed[:HALF]
    tile = packed[HALF:BLOCK]
    turned = tile.T
    first = jnp.where(rows <= cols, tile, turned)
    last = jnp.where(rows > cols, tile, jnp.where(rows < cols, turned, packed[BLOCK : BLOCK + 1]))
    return jnp.concatenate(
        [jnp.concatenate([first, off], axis=1), jnp.concatenate([off.T, last], axis=1)], axis=0
    )


def groups_of(rounds):
    return [(k,) for k in range(rounds - 2)] + [(rounds,), (rounds - 2,), (rounds - 1,)] if rounds > 3 else [(k,) for k in range(rounds + 1)]


def factor_of(scaled):
    rows = lax.broadcasted_iota(jnp.int32, (BLOCK, BLOCK), 0)
    cols = lax.broadcasted_iota(jnp.int32, (BLOCK, BLOCK), 1)
    return jnp.where(rows == cols, 1.25, 0.0) - scaled * 0.25


def advance_all(parts, scaled):
    squares = [split(product(p, p)) for p in parts]
    fourths = [product(p, p) for p in squares]
    return [product(split(f), split(m)) for f, m in zip(fourths, scaled)]


def root_open(statistics, scales, x_ref, m_ref):
    rows = lax.broadcasted_iota(jnp.int32, (BLOCK, BLOCK), 0)
    cols = lax.broadcasted_iota(jnp.int32, (BLOCK, BLOCK), 1)
    scaled, factors = [], []
    for i, (statistic, scale) in enumerate(zip(statistics, scales)):
        damped = statistic * scale + jnp.where(rows == cols, damping, 0.0)
        total = jnp.sum(jnp.sum(damped * damped, axis=0, keepdims=True), axis=1, keepdims=True)
        norm = jnp.sqrt(total)
        scaled.append(damped / norm)
        factors.append(factor_of(scaled[i]))
        x_ref[i] = factors[i] * lax.rsqrt(jnp.sqrt(norm))
    for i, value in enumerate(advance_all([split(f) for f in factors], scaled)):
        m_ref[i] = value


def root_steps(chains, count, x_ref, m_ref):
    def step(iteration, carry):
        scaled = [m_ref[i] for i in range(chains)]
        parts = [split(factor_of(m)) for m in scaled]
        for i in range(chains):
            x_ref[i] = product(split(x_ref[i]), parts[i])
        for i, value in enumerate(advance_all(parts, scaled)):
            m_ref[i] = value
        return carry

    for iteration in range(count):
        step(iteration, 0)


def root_close(chains, x_ref, m_ref):
    return [product(split(x_ref[i]), split(factor_of(m_ref[i]))) for i in range(chains)]


def kernel(
    sizes, g1_ref, g2_ref, out_ref, gh, gl, stage, rp, up, dn, rr, lp, lrecv, lr, own, x_ref, m_ref,
    load_sem, up_send, up_recv, dn_send, dn_recv, agu_send, agd_send, ag_recv,
    l_send, l_recv, lag_send, lag_recv,
):
    n, nl, rows, cols = sizes
    lcount, rcount = rows // BLOCK, cols // BLOCK
    M, ML = 2 * rcount, 2 * lcount
    K, KL = pl.cdiv(M, n), pl.cdiv(ML, nl)
    left_scale, right_scale = 1.0 / (cols * nl), 1.0 / (rows * n)
    z, c = lax.axis_index("row"), lax.axis_index("col")
    refs = (g1_ref, g2_ref)
    groups = groups_of(K)
    pairs = [group for group in groups if len(group) == 2]

    def load(step, block):
        slot = lax.rem(block, SLOTS)
        columns = pl.ds(pl.multiple_of(block * BLOCK, BLOCK), BLOCK)
        return pltpu.make_async_copy(
            refs[step].at[:, columns], stage.at[step, slot], load_sem.at[step, slot]
        )

    for block in range(min(SLOTS, rcount)):
        for step in range(2):
            load(step, block).start()

    def to_row(source, target, send, recv, row):
        return pltpu.make_async_remote_copy(
            source, target, send, recv, device_id=(row, c), device_id_type=MESH
        )

    def send_up(v, ref):
        return to_row(ref.at[v], up.at[v], up_send, up_recv.at[v], z + 1)

    def send_down(v, ref):
        return to_row(ref.at[v], dn.at[v], dn_send, dn_recv.at[v], z - 1)

    def root_up(v):
        return to_row(rr.at[v], rr.at[v], agu_send, ag_recv.at[v], z + 1)

    def root_down(v):
        return to_row(rr.at[v], rr.at[v], agd_send, ag_recv.at[v], z - 1)

    def left_out(w):
        return pltpu.make_async_remote_copy(
            lp.at[w], lrecv.at[w // nl, c], l_send, l_recv.at[w // nl, c],
            device_id=(z, lax.rem(w, nl)), device_id_type=MESH,
        )

    def left_in(kl, source):
        return pltpu.make_async_remote_copy(
            lp.at[0], lrecv.at[kl, source], l_send, l_recv.at[kl, source],
            device_id=(z, source), device_id_type=MESH,
        )

    def left_root(w, kl, other):
        return pltpu.make_async_remote_copy(
            lr.at[w], lr.at[w], lag_send, lag_recv.at[w],
            device_id=(z, other), device_id_type=MESH,
        )

    barrier = pltpu.get_barrier_semaphore()

    @pl.when(z > 0)
    def _():
        pl.semaphore_signal(barrier, inc=1, device_id=(z - 1, c), device_id_type=MESH)

    @pl.when(z < n - 1)
    def _():
        pl.semaphore_signal(barrier, inc=1, device_id=(z + 1, c), device_id_type=MESH)

    for d in range(1, nl):
        pl.semaphore_signal(
            barrier, inc=1, device_id=(z, lax.rem(c + d, nl)), device_id_type=MESH
        )
    def columns_of(block):
        return pl.ds(pl.multiple_of(block * BLOCK, BLOCK), BLOCK)

    def right_stat(block):
        slot = lax.rem(block, SLOTS)
        columns = columns_of(block)
        total = None
        for step in range(2):
            load(step, block).wait()
            high, low = split(stage[step, slot])
            gh[step, :, columns] = high
            gl[step, :, columns] = low
            turned = high.T
            cross = dot(turned, low)
            part = dot(turned, high) + (cross + cross.T)
            total = part if total is None else total + part
            pack(rp, 2 * block + step, total)

        @pl.when(block + SLOTS < rcount)
        def _():
            for step in range(2):
                load(step, block + SLOTS).start()

    def first_stat(block, carry):
        right_stat(block)
        return carry

    lax.fori_loop(0, FIRST, first_stat, 0)
    pl.semaphore_wait(barrier, nl - 1 + jnp.where(z > 0, 1, 0) + jnp.where(z < n - 1, 1, 0))

    def send_round(k):
        for d in range(1, n):
            up_unit, down_unit = k * n + n - d, k * n + d - 1

            @pl.when((z == 0) & (up_unit < M))
            def _():
                send_up(up_unit, rp).start()

            @pl.when((z == n - 1) & (down_unit < M))
            def _():
                send_down(down_unit, rp).start()

    def left_stat(block):
        lines = columns_of(block)
        total = None
        for step in range(2):
            high, low = gh[step, lines, :], gl[step, lines, :]
            cross = dot(high, low, NT)
            part = dot(high, high, NT) + (cross + cross.T)
            total = part if total is None else total + part
            pack(lp, 2 * block + step, total)

        for step in range(2):
            w = 2 * block + step

            @pl.when(lax.rem(w, nl) != c)
            def _():
                left_out(w).start()

    def relay_up(v):
        send_up(v, up).wait_recv()
        up[v] = up[v] + rp[v]
        send_up(v, up).start()

    def relay_down(v):
        send_down(v, dn).wait_recv()
        dn[v] = dn[v] + rp[v]
        send_down(v, dn).start()

    def gather(v):
        owner = lax.rem(v, n)

        @pl.when(owner < z)
        def _():
            root_up(v).wait_recv()

            @pl.when(z < n - 1)
            def _():
                root_up(v).start()

        @pl.when(owner > z)
        def _():
            root_down(v).wait_recv()

            @pl.when(z > 0)
            def _():
                root_down(v).start()

    def arrive(v):
        @pl.when(((z == 0) | (z == n - 1)) & (lax.rem(v, n) != z))
        def _():
            gather(v)

    def collect(k, slot):
        left = k >= K
        kl = k - K
        v, w = k * n + z, kl * nl + c

        @pl.when(jnp.logical_not(left) & (v < M))
        def _():
            own[slot] = rp[v]

            @pl.when(z > 0)
            def _():
                send_up(v, up).wait_recv()
                own[slot] = own[slot] + up[v]

            @pl.when(z < n - 1)
            def _():
                send_down(v, dn).wait_recv()
                own[slot] = own[slot] + dn[v]

        @pl.when(left & (w < ML))
        def _():
            own[slot] = lp[w]
            for d in range(1, nl):
                source = lax.rem(c + d, nl)
                left_in(kl, source).wait_recv()
                own[slot] = own[slot] + lrecv[kl, source]

    def scale_of(k):
        return jnp.where(k >= K, left_scale, right_scale)

    def deliver(k, result):
        left = k >= K
        kl = k - K
        v, w = k * n + z, kl * nl + c

        @pl.when(left & (w < ML))
        def _():
            pack(lr, w, result)
            for d in range(1, nl):
                left_root(w, kl, lax.rem(c + d, nl)).start()

        @pl.when(jnp.logical_not(left) & (v < M))
        def _():
            pack(rr, v, result)

            @pl.when(z < n - 1)
            def _():
                root_up(v).start()

            @pl.when(z > 0)
            def _():
                root_down(v).start()

    def members(item):
        first, second = jnp.int32(pairs[0][0]), jnp.int32(pairs[0][1])
        for j in range(1, len(pairs)):
            first = jnp.where(item == j, pairs[j][0], first)
            second = jnp.where(item == j, pairs[j][1], second)
        return first, second

    def opening(ks):
        for slot, k in enumerate(ks):
            collect(k, slot)
        root_open([unpack(own[slot]) for slot in range(len(ks))], [scale_of(k) for k in ks], x_ref, m_ref)

    def closing(ks):
        for k, result in zip(ks, root_close(len(ks), x_ref, m_ref)):
            deliver(k, result)

    def open_one(k):
        opening((k,))

    def steps_one(item):
        root_steps(1, (ITERS - 2) // SEGMENTS, x_ref, m_ref)

    def close_one(k):
        closing((k,))

    def open_two(item):
        opening(members(item))

    def steps_two(item):
        root_steps(2, (ITERS - 2) // SEGMENTS, x_ref, m_ref)

    def close_two(item):
        closing(members(item))

    width, pieces = cols, 1

    def left_apply(w):
        @pl.when(lax.rem(w, nl) != c)
        def _():
            left_root(w, 0, lax.rem(w, nl)).wait_recv()

        step = lax.rem(w, 2)
        lines = columns_of(w // 2)
        factor = split(unpack(lr[w]))

        def piece(t, inner):
            columns = pl.ds(pl.multiple_of(t * width, HALF), width)
            high, low = gh[step, lines, columns], gl[step, lines, columns]
            high, low = split(product(factor, (high, low)))
            gh[step, lines, columns] = high
            gl[step, lines, columns] = low
            return inner

        lax.fori_loop(0, pieces, piece, 0)

    def right_apply(block):
        columns = columns_of(block)
        arrive(2 * block)
        arrive(2 * block + 1)
        lefts, rights = [], []
        for step in range(2):
            high, low = split(unpack(rr[2 * block + step]))
            grad_high, grad_low = gh[step, :, columns], gl[step, :, columns]
            lefts += [grad_high, grad_high, grad_low]
            rights += [high, low, high]
        out_ref[:, columns] = dot(jnp.concatenate(lefts, axis=1), jnp.concatenate(rights, axis=0))

    work = {
        STAT: right_stat, SEND: send_round, LEFT: left_stat, UP: relay_up, DOWN: relay_down,
        GATHER: gather, OPEN: open_one, STEPS: steps_one, ROOT: close_one,
        OPEN2: open_two, STEPS2: steps_two, ROOT2: close_two, LAPPLY: left_apply, RAPPLY: right_apply,
    }
    programs = plan(n, K, M, ML, rcount, lcount, groups)
    used = sorted({kind for program in programs for kind, _ in program} & set(work))
    weight = {name: sum(kind == name for p in programs for kind, _ in p) for name in used}
    digit = 16
    while digit < 16 * max(M, ML, K + KL, rcount):
        digit *= 2
    held = max(h for h in (1, 2, 3) if digit**h < 2**31)
    lists = []
    for program in programs:
        program = program + [(NOP, 0)] * (-len(program) % held)
        codes = [item * 16 + kind for kind, item in program]
        lists.append(
            [sum(code * digit**j for j, code in enumerate(codes[i : i + held])) for i in range(0, len(codes), held)]
        )

    def of_row(values):
        value = jnp.int32(values[0])
        for row in range(1, n):
            value = jnp.where(z == row, values[row], value)
        return value

    longest = max(len(words) for words in lists)
    words = [of_row([w[i] if i < len(w) else 0 for w in lists]) for i in range(longest)]
    last = of_row([len(w) for w in lists])

    def look_up(values, index, width):
        if len(values) == 1:
            return values[0]
        half = width // 2
        low = look_up(values[:half], index, half)
        if len(values) <= half:
            return low
        return jnp.where(lax.rem(index, width) >= half, look_up(values[half:], index, half), low)

    def choose(kind, names):
        if len(names) == 1:
            return work[names[0]]
        weights = [weight[name] for name in names]
        middle = min(
            range(1, len(names)), key=lambda m: abs(sum(weights[:m]) - sum(weights[m:]))
        )
        low, high = choose(kind, names[:middle]), choose(kind, names[middle:])

        def act(item):
            @pl.when(kind < names[middle])
            def _():
                low(item)

            @pl.when(kind >= names[middle])
            def _():
                high(item)

        return act

    def turn(index, carry):
        width = 1
        while width < longest:
            width *= 2

        def task(j, word):
            code = lax.rem(word, digit)
            kind, item = lax.rem(code, 16), lax.div(code, 16)

            @pl.when(kind != NOP)
            def _():
                choose(kind, used)(item)

            return lax.div(word, digit)

        lax.fori_loop(0, held, task, look_up(words, index, width))
        return carry

    lax.fori_loop(0, last, turn, 0)

    def sent(ref, sem, count):
        if count:
            whole = ref.at[pl.ds(0, count)]
            to_row(whole, whole, sem, ag_recv.at[0], z).wait_send()

    for row in range(n):
        @pl.when(z == row)
        def _():
            owners = [v % n for v in range(M)]
            if row < n - 1:
                sent(up, up_send, sum(owner > row for owner in owners))
                sent(rr, agu_send, sum(owner <= row for owner in owners))
            if row > 0:
                sent(dn, dn_send, sum(owner < row for owner in owners))
                sent(rr, agd_send, sum(owner >= row for owner in owners))

    def left_sent(own_count):
        sent(lp, l_send, ML - own_count)
        sent(lrecv.at[0], lag_send, own_count * (nl - 1))

    if ML % nl:
        @pl.when(c < ML % nl)
        def _():
            left_sent(ML // nl + 1)

        @pl.when(c >= ML % nl)
        def _():
            left_sent(ML // nl)
    else:
        left_sent(ML // nl)


def body(n, nl, grad_first, grad_second):
    rows, cols = grad_first.shape
    lcount, rcount = rows // BLOCK, cols // BLOCK
    M, ML = 2 * rcount, 2 * lcount
    K, KL = pl.cdiv(M, n), pl.cdiv(ML, nl)
    f32, bf16 = jnp.float32, jnp.bfloat16
    unit = (PACKED, HALF)
    dma = pltpu.SemaphoreType.DMA
    return pl.pallas_call(
        functools.partial(kernel, (n, nl, rows, cols)),
        in_specs=[pl.BlockSpec(memory_space=pl.ANY)] * 2,
        out_specs=pl.BlockSpec(memory_space=pltpu.VMEM),
        out_shape=pltpu.VMEM((rows, cols), f32),
        scratch_shapes=[
            pltpu.VMEM((2, rows, cols), bf16),
            pltpu.VMEM((2, rows, cols), bf16),
            pltpu.VMEM((2, SLOTS, rows, BLOCK), f32),
            pltpu.VMEM((M, *unit), f32),
            pltpu.VMEM((M, *unit), f32),
            pltpu.VMEM((M, *unit), f32),
            pltpu.VMEM((M, *unit), f32),
            pltpu.VMEM((ML, *unit), f32),
            pltpu.VMEM((KL, nl, *unit), f32),
            pltpu.VMEM((ML, *unit), f32),
            pltpu.VMEM((2, *unit), f32),
            pltpu.VMEM((2, BLOCK, BLOCK), f32),
            pltpu.VMEM((2, BLOCK, BLOCK), f32),
            dma((2, SLOTS)),
            dma,
            dma((M,)),
            dma,
            dma((M,)),
            dma,
            dma,
            dma((M,)),
            dma,
            dma((KL, nl)),
            dma,
            dma((ML,)),
        ],
        compiler_params=pltpu.CompilerParams(
            collective_id=0, has_side_effects=True, vmem_limit_bytes=VMEM_LIMIT
        ),
    )(grad_first, grad_second)


def solution(mesh):
    spec = P("row", "col")
    return jax.shard_map(
        functools.partial(body, mesh.shape["row"], mesh.shape["col"]),
        mesh=mesh,
        in_specs=(spec, spec),
        out_specs=spec,
        check_vma=False,
    )
```
